128 devices in a mesh: rows: 16 (over x, z), mlp: 8 (over y, core).
Axes of the slice: x: 4, y: 4, z: 4, core: 2. Of those that a mesh axis runs over, the one named last changes fastest.
Arguments:
- tokens: bfloat16 [32768, 1408], P(('rows', 'mlp')), may hold values from -6 to 6
- norm_gain: float32 [3, 1408], replicated, may hold values from 0.1 to 1.9
- norm_bias: float32 [3, 1408], replicated, may hold values from -2 to 2
- input_weight: bfloat16 [1408, 4224], replicated, may hold values from -0.15625 to 0.15625
- input_bias: float32 [4224], replicated, may hold values from -36 to 36
- output_weight: bfloat16 [1408, 1408], replicated, may hold values from -0.15625 to 0.15625
- expand_weight: bfloat16 [6144, 1408], P('rows'), may hold values from -0.15625 to 0.15625
- reduce_weight: bfloat16 [6144, 1408], P('rows'), may hold values from -0.078125 to 0.078125
- merger_weight: bfloat16 [5632, 4096], P(None, 'mlp'), may hold values from -1 to 1
- output_gain: float32 [4096], P('mlp'), may hold values from 0.1 to 1.9
- segments: int32 [32768], P(('rows', 'mlp')), may hold values from 0 to 4, as said below
- grid_sides: int32 [512, 2], P('rows'), may hold values from 0 to 8, as said below
- routes: int32 [8192, 1], P('rows'), may hold values from 0 to 127; in each aligned block of 512 rows (0 to 511, 512 to 1023, ...) at most 8 rows name the same one
Outputs:
- delivered: bfloat16 [16384, 4096], P(('rows', 'mlp'))
- peaks: float32 [512], P(('rows', 'mlp'))
The draws below stay inside these ranges and needn't reach their ends.
Inputs may be any that keep to these rules, and one draw needn't show every extreme that they name: `grid_sides`: every device has 4 request slots; a present request has even height and width of 2 to 8, an absent slot 0 and 0; each device holds 1 to 4 requests, whose 1 + height * width tokens together fit in its 256 token slots; some request is 8 x 8. A device's tokens hold its present requests in slot order from its first token on, each as a class token followed by its height x width patches in row-major order; segments gives the slot number of each such token and 4 for the remaining padding tokens. `routes`: in each aligned block of 512 merged rows (the merged rows of 8 consecutive devices) no destination is named more than 8 times; in some block some destination is named exactly 8 times. Zero merged rows have destinations too.
All inputs are finite; a program needn't handle non-finite values.
Results may differ from the reference program's by a relative error of at most 0.012.
The reference program's roundings to bfloat16 on the way count: a program that leaves them out, or rounds other values in their place, can miss the bound.
Values may be sent and summed in bfloat16 or wider, within the bound.
A program may use at most 192 MiB of HBM per device.

```python
import math
import jax
import jax.numpy as jnp
import numpy as np
from jax import lax

D = 1408
HEADS = 16
HEAD = 88
FF = 6144
OUT = 4096
TOK_DEV = 256
SIDE = 8
REQ_DEV = 4
MERGED_DEV = 64
CAP = 8
TOKENS = 32768
MERGED = 8192
N_ROWS = 16
N_MLP = 8


def request_sides(key):
    devices = N_ROWS * N_MLP
    base = jax.random.fold_in(key, 11)
    key_big, key_small, key_present, key_order = jax.random.split(base, 4)
    big = 2 * jax.random.randint(key_big, (devices, 1, 2), SIDE // 4, SIDE // 2 + 1)
    first_device = (jnp.arange(devices) == 0)[:, None, None]
    big = jnp.where(first_device, SIDE, big)
    small = 2 * jax.random.randint(key_small, (devices, REQ_DEV - 1, 2), 1, SIDE // 4 + 1)
    present = (jax.random.randint(key_present, (devices, REQ_DEV - 1, 1), 0, 4) > 0).astype(jnp.int32)
    sides = jnp.concatenate([big, small * present], axis=1).astype(jnp.int32)
    ranking = jax.random.randint(key_order, (devices, REQ_DEV), 0, 1 << 20) * REQ_DEV + jnp.arange(REQ_DEV)
    slot_order = jnp.argsort(ranking, axis=1)
    return jnp.take_along_axis(sides, slot_order[:, :, None], axis=1).astype(jnp.int32)


def draw_grid_sides(key, part):
    sides = request_sides(key)
    return sides.reshape(N_ROWS * N_MLP * REQ_DEV, 2).astype(jnp.int32)


def draw_segments(key, part):
    sides = request_sides(key)
    heights = sides[:, :, 0]
    widths_all = sides[:, :, 1]
    lengths = jnp.where(heights > 0, 1 + heights * widths_all, 0)
    starts = jnp.cumsum(lengths, axis=1) - lengths
    positions = jnp.arange(TOK_DEV)
    inside = (positions[None, None, :] >= starts[:, :, None]) & (positions[None, None, :] < (starts + lengths)[:, :, None])
    slot_ids = jnp.arange(REQ_DEV)[None, :, None]
    labels = jnp.sum(jnp.where(inside, slot_ids, 0), axis=1)
    labels = labels + REQ_DEV * (1 - jnp.any(inside, axis=1).astype(jnp.int32))
    return labels.reshape(-1).astype(jnp.int32)


def draw_input_bias(key, part):
    key_base = jax.random.fold_in(jax.random.fold_in(key, 5), 0)
    bias = jnp.clip(0.5 * jax.random.normal(key_base, (3 * D,), jnp.float32), -2.0, 2.0)
    return bias.astype(jnp.float32)


def draw_merger_weight(key, part):
    key_values, key_jitter = jax.random.split(jax.random.fold_in(key, 3))
    column = jnp.arange(OUT, dtype=jnp.float32) / OUT
    jitter = jax.random.uniform(key_jitter, (OUT,), jnp.float32, minval=-0.5, maxval=0.5)
    column_scale = jnp.exp(2.302585 * (column - 0.5 + jitter))
    values = jnp.clip(jax.random.normal(key_values, (4 * D, OUT), jnp.float32), -6.0, 6.0)
    scaled = values * column_scale[None, :] / jnp.sqrt(jnp.float32(4 * D))
    scaled = jnp.clip(scaled, -1.0, 1.0)
    return scaled.astype(jnp.bfloat16)


def block_scale(rng, dims, cuts, least, largest):
    level, own = 1.0, jax.random.fold_in(rng, 6)
    for axis_at, shards_of in cuts:
        steps = jnp.exp(jax.random.uniform(jax.random.fold_in(own, axis_at), (shards_of,), jnp.float32, least / len(cuts), largest / len(cuts)))
        level = level * jnp.repeat(steps, dims[axis_at] // shards_of).reshape([-1 if axis == axis_at else 1 for axis in range(len(dims))])
    return level


def shared_out(own_key, own, number, rows, amount, top, limit, slope):
    order = jax.random.permutation(own_key, amount)
    heavy_load, common = load_shares(amount, rows * top, limit, slope, True), load_shares(amount, rows * top, limit, slope, False)
    places = jnp.arange(amount)

    def named(sizes, rotation):
        used = int((sizes > 0).sum())
        fixed = max(1, used // 4)
        passed = fixed + (places - fixed + rotation * (used - fixed)) % max(1, amount - fixed)
        return jnp.zeros((amount,), jnp.int32).at[order[jnp.where(places < fixed, places, passed)]].set(jnp.asarray(sizes, jnp.int32))

    sizes = jnp.where(number % 4 == 0, named(heavy_load, number // 4), named(common, number - number // 4 - 1))
    mixed = jax.random.permutation(jax.random.fold_in(own, 3), amount)
    source_of, taker = mixed[0:amount // 2 * 2:2], mixed[1:amount // 2 * 2:2]
    margin = jnp.minimum(sizes[source_of] - 1, limit - sizes[taker]) // 2
    margin = jnp.where((source_of == order[0]) | (taker == order[0]) | (sizes[taker] == 0), 0, jnp.maximum(margin, 0))
    passed = jax.random.randint(jax.random.fold_in(own, 4), (amount // 2,), 0, 1 << 20) % (margin + 1)
    sizes = sizes.at[source_of].add(-passed).at[taker].add(passed)
    members = jnp.searchsorted(jnp.cumsum(sizes), jnp.arange(rows * top), side="right").astype(jnp.int32)
    table = members.reshape(top, rows).T
    table = table[jax.random.permutation(jax.random.fold_in(own, 1), rows)]
    rotation = jax.random.randint(jax.random.fold_in(own, 2), (rows, 1), 0, top)
    return jnp.take_along_axis(table, (jnp.arange(top)[None, :] + rotation) % top, axis=1)


def load_shares(amount, total, limit, skew, full):
    weights = [(1 << 20) // math.isqrt(standing ** skew) + 1 for standing in range(1, amount + 1)]
    largest = limit if full else min(limit, max(-(-total // amount), total * weights[0] // sum(weights)))
    least = 1 if total - largest >= amount - 1 else 0
    holding, surplus = [largest] + [least] * (amount - 1), total - largest - least * (amount - 1)
    while surplus > 0:
        free = [i for i in range(1, amount) if holding[i] < largest] or [i for i in range(1, amount) if holding[i] < limit]
        mass, remaining = sum([weights[i] for i in free]), surplus
        for i in free:
            more = min(limit - holding[i], max(1, remaining * weights[i] // mass), surplus)
            holding[i] = holding[i] + more
            surplus = surplus - more
    return np.array(holding)


def bell_draw(own_key, dims, spread, reach, cuts=(), held_as=jnp.bfloat16):
    entries = spread * jax.random.normal(own_key, dims, jnp.float32)
    if cuts:
        entries = entries * block_scale(own_key, dims, cuts, -0.22, 0.18)
    return jnp.clip(entries, -reach, reach).astype(held_as)


def setup_inputs(seed: int = 0) -> dict:
    streams_of = jax.random.split(jax.random.key(seed), 14)
    tokens = bell_draw(streams_of[0], (TOKENS, D), 1.0, 6.0, ((0, 128),))
    norm_gain = jnp.clip(1.0 + 0.18 * jax.random.normal(streams_of[1], (3, D), jnp.float32), 0.1, 1.9)
    norm_bias = bell_draw(streams_of[2], (3, D), 0.3, 2.0, (), jnp.float32)
    input_weight = bell_draw(streams_of[3], (D, 3 * D), D ** -0.5, 0.15625)
    input_bias = draw_input_bias(jax.random.fold_in(streams_of[13], 71), 0)
    output_weight = bell_draw(streams_of[5], (D, D), D ** -0.5, 0.15625)
    expand_weight = bell_draw(streams_of[6], (FF, D), D ** -0.5, 0.15625, ((0, 16),))
    reduce_weight = bell_draw(streams_of[7], (FF, D), FF ** -0.5, 0.078125, ((0, 16),))
    merger_weight = draw_merger_weight(jax.random.fold_in(streams_of[13], 71), 0)
    output_gain = jnp.clip(1.0 + 0.18 * jax.random.normal(streams_of[9], (OUT,), jnp.float32), 0.1, 1.9)
    segments = draw_segments(jax.random.fold_in(streams_of[13], 71), 0)
    grid_sides = draw_grid_sides(jax.random.fold_in(streams_of[13], 71), 0)
    routes_keys = jax.random.split(jax.random.fold_in(streams_of[12], 1), MERGED // (N_MLP * MERGED_DEV))
    routes_turns = jax.random.permutation(jax.random.fold_in(streams_of[12], 3), MERGED // (N_MLP * MERGED_DEV))
    routes = jax.vmap(lambda own, number: shared_out(jax.random.fold_in(streams_of[12], 2), own, number, N_MLP * MERGED_DEV, N_ROWS * N_MLP, 1, CAP, 2))(routes_keys, routes_turns).reshape((MERGED, 1))
    return dict(tokens=tokens, norm_gain=norm_gain, norm_bias=norm_bias, input_weight=input_weight, input_bias=input_bias, output_weight=output_weight, expand_weight=expand_weight, reduce_weight=reduce_weight, merger_weight=merger_weight, output_gain=output_gain, segments=segments, grid_sides=grid_sides, routes=routes)


EPS = 1e-06

def layer_norm(values, gain, bias):
    mean_value = lax.optimization_barrier(jnp.mean(values, axis=-1, keepdims=True))
    centered = values - mean_value
    variance = lax.optimization_barrier(jnp.mean(centered * centered, axis=-1, keepdims=True))
    return centered * lax.rsqrt(variance + EPS) * gain + bias

def merge_layout(grid_block):
    heights = grid_block[:, 0]
    widths_all = grid_block[:, 1]
    lengths = jnp.where(heights > 0, 1 + heights * widths_all, 0).astype(jnp.int32)
    starts = (jnp.cumsum(lengths) - lengths).astype(jnp.int32)
    counts = (heights // 2 * (widths_all // 2)).astype(jnp.int32)
    merge_starts = (jnp.cumsum(counts) - counts).astype(jnp.int32)
    merge_ends = merge_starts + counts
    merge_slots = jnp.arange(MERGED_DEV, dtype=jnp.int32)
    owner_slot = lax.optimization_barrier(jnp.sum((merge_ends[None, :] <= merge_slots[:, None]).astype(jnp.int32), axis=1)).astype(jnp.int32)
    is_valid = owner_slot < REQ_DEV
    chosen = (owner_slot[:, None] == jnp.arange(REQ_DEV, dtype=jnp.int32)[None, :]).astype(jnp.int32)
    row_width = lax.optimization_barrier(jnp.sum(chosen * widths_all[None, :], axis=1)).astype(jnp.int32)
    row_start = lax.optimization_barrier(jnp.sum(chosen * starts[None, :], axis=1)).astype(jnp.int32)
    row_merge = lax.optimization_barrier(jnp.sum(chosen * merge_starts[None, :], axis=1)).astype(jnp.int32)
    within = merge_slots - row_merge
    half_width = jnp.maximum(row_width // 2, 1)
    patch_row = within // half_width
    patch_col = within - patch_row * half_width
    corner = row_start + 1 + 2 * patch_row * row_width + 2 * patch_col
    token_index = jnp.stack([corner, corner + 1, corner + row_width, corner + row_width + 1], axis=1)
    token_index = jnp.where(is_valid[:, None], token_index, 0).astype(jnp.int32)
    return (token_index, is_valid, owner_slot, counts)

def reference(tokens, norm_gain, norm_bias, input_weight, input_bias, output_weight, expand_weight, reduce_weight, merger_weight, output_gain, segments, grid_sides, routes):
    devices = N_ROWS * N_MLP
    features = tokens.shape[1]
    residual_in = tokens.astype(jnp.float32)
    normed_in = layer_norm(residual_in, norm_gain[0], norm_bias[0]).astype(jnp.bfloat16)
    joint = (jnp.dot(normed_in, input_weight, preferred_element_type=jnp.float32) + input_bias).astype(jnp.bfloat16)

    def attend(pair):
        block_rows, block_segments = pair
        queries = block_rows[:, :features].astype(jnp.float32).reshape(TOK_DEV, HEADS, HEAD)
        keys_all = block_rows[:, features:2 * features].astype(jnp.float32).reshape(TOK_DEV, HEADS, HEAD)
        values_all = block_rows[:, 2 * features:].astype(jnp.float32).reshape(TOK_DEV, HEADS, HEAD)
        scores = jnp.einsum('thd,uhd->htu', queries, keys_all) / math.sqrt(HEAD)
        allowed = block_segments[:, None] == block_segments[None, :]
        scores = jnp.where(allowed[None], scores, -jnp.inf)
        row_max = lax.optimization_barrier(jnp.max(scores, axis=-1, keepdims=True))
        weights = jnp.exp(scores - row_max)
        softmax_out = (weights / lax.optimization_barrier(jnp.sum(weights, axis=-1, keepdims=True))).astype(jnp.bfloat16)
        mixed = jnp.einsum('htu,uhd->thd', softmax_out.astype(jnp.float32), values_all)
        return mixed.astype(jnp.bfloat16).reshape(TOK_DEV, features)
    attended = lax.map(attend, (joint.reshape(devices, TOK_DEV, 3 * features), segments.reshape(devices, TOK_DEV)))
    attended = attended.reshape(devices * TOK_DEV, features)
    residual_mid = residual_in + jnp.dot(attended, output_weight, preferred_element_type=jnp.float32)
    normed_mid = layer_norm(residual_mid, norm_gain[1], norm_bias[1]).astype(jnp.bfloat16)
    pre_act = jnp.dot(normed_mid, expand_weight.T, preferred_element_type=jnp.float32)
    hidden = jax.nn.gelu(pre_act, approximate=False).astype(jnp.bfloat16)
    residual_out = residual_mid + jnp.dot(hidden, reduce_weight, preferred_element_type=jnp.float32)
    normed_out = layer_norm(residual_out, norm_gain[2], norm_bias[2]).astype(jnp.bfloat16)
    token_index, is_valid, owner_slot, counts = jax.vmap(merge_layout)(grid_sides.reshape(devices, REQ_DEV, 2))

    def pick_rows(rows_block, index_block):
        return jnp.take(rows_block, index_block.reshape(-1), axis=0)
    picked = jax.vmap(pick_rows)(normed_out.reshape(devices, TOK_DEV, features), token_index)
    picked = picked.reshape(devices * MERGED_DEV, 4 * features)
    valid_rows = is_valid.reshape(-1)
    merged = jnp.where(valid_rows[:, None], picked, jnp.zeros_like(picked)).astype(jnp.bfloat16)
    projected = jnp.dot(merged, merger_weight, preferred_element_type=jnp.float32)
    gained = projected * output_gain
    requests = devices * REQ_DEV
    device_base = (REQ_DEV * jnp.arange(devices, dtype=jnp.int32))[:, None]
    request_of_row = jnp.where(is_valid, owner_slot + device_base, requests).reshape(-1).astype(jnp.int32)
    square_sum = jax.ops.segment_sum(lax.optimization_barrier(jnp.sum(projected * projected, axis=1)), request_of_row, num_segments=requests + 1)[:requests]
    peak_all = jax.ops.segment_max(lax.optimization_barrier(jnp.max(gained, axis=1)), request_of_row, num_segments=requests + 1)[:requests]
    counts = counts.reshape(-1)
    inv_rms = lax.rsqrt(square_sum / (jnp.maximum(counts, 1).astype(jnp.float32) * OUT) + EPS)
    row_inv = jnp.where(valid_rows, inv_rms[jnp.minimum(request_of_row, requests - 1)], jnp.zeros_like(inv_rms[0]))
    scaled = (gained * row_inv[:, None]).astype(jnp.bfloat16)
    peaks = jnp.where(counts > 0, peak_all * inv_rms, jnp.zeros_like(inv_rms))
    targets = routes[:, 0].astype(jnp.int32)
    group_rows = N_MLP * MERGED_DEV

    def rank_block(block_targets):
        row_order = jnp.arange(group_rows, dtype=jnp.int32)
        same_target = (block_targets[:, None] == block_targets[None, :]) & (row_order[None, :] < row_order[:, None])
        return lax.optimization_barrier(jnp.sum(same_target.astype(jnp.int32), axis=1)).astype(jnp.int32)
    target_rank = lax.map(rank_block, targets.reshape(N_ROWS, group_rows)).reshape(-1)
    group_of_row = (jnp.arange(devices * MERGED_DEV, dtype=jnp.int32) // group_rows).astype(jnp.int32)
    position = targets * (CAP * N_ROWS) + target_rank * N_ROWS + group_of_row
    delivered = jnp.zeros((devices * CAP * N_ROWS, OUT), jnp.bfloat16).at[position].set(scaled)
    return (delivered, peaks)
```

```python
import math

import jax
import jax.numpy as jnp
from jax import lax
from jax.experimental import pallas as pl
from jax.experimental.pallas import tpu as pltpu
from jax.sharding import PartitionSpec as P

HEADS = 16
HEAD = 88
OUT = 4096
REQ_DEV = 4
MERGED_DEV = 64


EPS = 1e-06


def combined_all(part, axis, combine):
    gathered = jax.tree.map(lambda a: lax.all_gather(a, axis), part)

    def take(source):
        return jax.tree.map(lambda a: lax.dynamic_index_in_dim(a, source, 0, False), gathered)

    return lax.fori_loop(
        1, lax.axis_size(axis), lambda source, state: combine(state, take(source)), take(0)
    )


def merge_layout(grid_block):
    heights = grid_block[:, 0]
    widths_all = grid_block[:, 1]
    lengths = jnp.where(heights > 0, 1 + heights * widths_all, 0)
    starts = jnp.cumsum(lengths) - lengths
    counts = heights // 2 * (widths_all // 2)
    merge_starts = jnp.cumsum(counts) - counts
    merge_ends = merge_starts + counts
    merge_slots = jnp.arange(MERGED_DEV, dtype=jnp.int32)
    owner_slot = jnp.sum((merge_ends[None, :] <= merge_slots[:, None]).astype(jnp.int32), axis=1)
    is_valid = owner_slot < REQ_DEV
    chosen = (owner_slot[:, None] == jnp.arange(REQ_DEV, dtype=jnp.int32)[None, :]).astype(
        jnp.int32
    )
    row_width = jnp.sum(chosen * widths_all[None, :], axis=1)
    row_start = jnp.sum(chosen * starts[None, :], axis=1)
    row_merge = jnp.sum(chosen * merge_starts[None, :], axis=1)
    within = merge_slots - row_merge
    half_width = jnp.maximum(row_width // 2, 1)
    patch_row = within // half_width
    patch_col = within - patch_row * half_width
    corner = row_start + 1 + 2 * patch_row * row_width + 2 * patch_col
    token_index = jnp.stack(
        [corner, corner + 1, corner + row_width, corner + row_width + 1], axis=1
    )
    token_index = jnp.where(is_valid[:, None], token_index, 0)
    return (token_index, is_valid, owner_slot, counts)


def combine_totals(earlier, latter):
    return (earlier[0] + latter[0], jnp.maximum(earlier[1], latter[1]))


MESH = pl.DeviceIdType.MESH
PLANE = 144
HALF = 80
SHARE = 16
SLOT = 192


def layer_kernel(
    tokens, gain, bias, wq_hbm, bq, wo_hbm, wa_hbm, wb_hbm, seg, idx, merged_out,
    wa, wb, wq, wo, joint, acts, resid, acc, att, maskb, psend, precv,
    send, recv, local,
):
    row = lax.axis_index("rows")
    member = lax.axis_index("mlp")
    x, z = row // 4, row % 4
    y, core = member // 2, member % 2
    features = tokens.shape[1]
    rows_here = tokens.shape[0]

    def plane(dx, dz):
        return (((x + dx + 4) % 4) * 4 + (z + dz + 4) % 4, member)

    def column(dy):
        return (row, ((y + dy + 4) % 4) * 2 + core)

    partner = (row, member + 1 - 2 * core)
    near = [plane(1, 0), plane(-1, 0), plane(0, 1), plane(0, -1), column(1), column(-1), partner]

    started = []

    def load(src, dst):
        copy = pltpu.make_async_copy(src, dst, local.at[len(started)])
        copy.start()
        started.append(copy)
        return copy

    own = []
    first = SLOT - 4 * SHARE
    for hbm, vmem in ((wa_hbm, wa), (wb_hbm, wb)):
        base = pl.multiple_of(core * SLOT, 16)
        own.append(load(hbm.at[pl.ds(base, first)], vmem.at[0, 0, pl.ds(0, first)]))
        for place, offset in enumerate((0, -1, 1, 2)):
            at = pl.multiple_of(core * SLOT + first + SHARE * ((y + offset + 4) % 4), 16)
            own.append(
                load(hbm.at[pl.ds(at, SHARE)], vmem.at[0, 0, pl.ds(first + place * SHARE, SHARE)])
            )
    chunk = 384
    parts = wq_hbm.shape[1] // chunk
    first_wq = len(started)
    for j in range(parts):
        load(wq_hbm.at[:, pl.ds(j * chunk, chunk)], wq.at[:, pl.ds(j * chunk, chunk)])
    wo_copy = load(wo_hbm, wo)

    barrier = pltpu.get_barrier_semaphore()
    for device in near:
        pl.semaphore_signal(barrier, inc=1, device_id=device, device_id_type=MESH)
    pl.semaphore_wait(barrier, len(near))

    sent = []

    def push(src, dst, device):
        k = len(sent)
        copy = pltpu.make_async_remote_copy(
            src_ref=src, dst_ref=dst, send_sem=send.at[k], recv_sem=recv.at[k],
            device_id=device, device_id_type=MESH,
        )
        copy.start()
        sent.append(copy)
        return copy

    def slot_a(i, k):
        return wa.at[k, i]

    def slot_b(i, k):
        return wb.at[i, k]

    def step_x(s):
        return plane(s, 0)

    def step_z(s):
        return plane(0, s)

    weights = ((slot_a, step_x, step_z), (slot_b, step_z, step_x))
    up, low, whole = pl.ds(0, HALF), pl.ds(HALF, PLANE - HALF), pl.ds(0, PLANE)

    def send_first(w):
        slot, one, _ = w
        return [
            push(slot(0, 0).at[whole], slot(3, 0).at[whole], one(1)),
            push(slot(0, 0).at[whole], slot(1, 0).at[whole], one(-1)),
        ]

    def forward_first(w):
        slot, one, _ = w
        return [
            push(slot(3, 0).at[up], slot(2, 0).at[up], one(1)),
            push(slot(1, 0).at[low], slot(2, 0).at[low], one(-1)),
        ]

    def send_second(w, i):
        slot, _, two = w
        return [
            push(slot(i, 0).at[whole], slot(i, 3).at[whole], two(1)),
            push(slot(i, 0).at[whole], slot(i, 1).at[whole], two(-1)),
        ]

    def forward_second(w, i):
        slot, _, two = w
        return [
            push(slot(i, 3).at[up], slot(i, 2).at[up], two(1)),
            push(slot(i, 1).at[low], slot(i, 2).at[low], two(-1)),
        ]

    share = [pl.ds(first + j * SHARE, SHARE) for j in range(4)]

    def share_out(w, i, k):
        slot = w[0]
        return [
            push(slot(i, k).at[share[0]], slot(i, k).at[share[1]], column(1)),
            push(slot(i, k).at[share[0]], slot(i, k).at[share[2]], column(-1)),
        ]

    def share_on(w, i, k):
        slot = w[0]
        if (i + k) % 2 == 0:
            return push(slot(i, k).at[share[1]], slot(i, k).at[share[3]], column(1))
        return push(slot(i, k).at[share[2]], slot(i, k).at[share[3]], column(-1))

    def arrived(copies):
        for copy in copies:
            copy.wait_recv()

    for copy in own:
        copy.wait()
    table = {}
    for n, w in enumerate(weights):
        table["s1", n] = send_first(w)
    for n, w in enumerate(weights):
        table["s2", n, 0] = send_second(w, 0)

    passing = []

    def spread(slots):
        for n, i, k in slots:
            passing.append((n, i, k, share_out(weights[n], i, k)))

    final = []

    def pass_on(count):
        for _ in range(min(count, len(passing))):
            n, i, k, copies = passing.pop(0)
            arrived(copies)
            final.append(share_on(weights[n], i, k))

    def service_first():
        for n in (0, 1):
            arrived(table["s1", n])
        for n in (0, 1):
            table["f1", n] = forward_first(weights[n])
        for n in (0, 1):
            for i in (1, 3):
                table["s2", n, i] = send_second(weights[n], i)
        spread([(n, i, 0) for n in (0, 1) for i in (1, 3)])

    def service_second(i):
        for n in (0, 1):
            arrived(table["s2", n, i])
            table["f2", n, i] = forward_second(weights[n], i)
        spread([(n, i, k) for n in (0, 1) for k in (1, 3)])

    def service_across():
        for n in (0, 1):
            arrived(table["f1", n])
            table["s2", n, 2] = send_second(weights[n], 2)
        spread([(n, 2, 0) for n in (0, 1)])

    def service_last(i):
        for n in (0, 1):
            arrived(table["f2", n, i])
        spread([(n, i, 2) for n in (0, 1)])

    def norm_rows(read, write, i):
        def body(t, carry):
            at = pl.ds(pl.multiple_of(t * 32, 32), 32)
            value = read(at)
            mean = jnp.mean(value, axis=-1, keepdims=True)
            centered = value - mean
            variance = jnp.mean(centered * centered, axis=-1, keepdims=True)
            write(at, centered * lax.rsqrt(variance + EPS) * gain[i : i + 1, :] + bias[i : i + 1, :])
            return carry

        lax.fori_loop(0, rows_here // 32, body, 0)

    def write_acts(at, value):
        acts[at, :] = value.astype(jnp.bfloat16)

    norm_rows(lambda at: tokens[at, :].astype(jnp.float32), write_acts, 0)
    seg_f = jnp.broadcast_to(seg[...].astype(jnp.float32), (rows_here, rows_here))
    maskb[...] = jnp.where(seg_f == seg_f.T, 0.0, -jnp.inf)
    joint[:, parts * chunk :] = jnp.zeros((rows_here, joint.shape[1] - parts * chunk), jnp.bfloat16)
    att[...] = jnp.zeros_like(att)

    def project(j, carry):
        cols = pl.ds(pl.multiple_of(j * chunk, chunk), chunk)
        pltpu.make_async_copy(wq_hbm.at[:, cols], wq.at[:, cols], local.at[first_wq + j]).wait()
        value = jnp.dot(acts[0:rows_here, :], wq[:, cols], preferred_element_type=jnp.float32)
        joint[:, cols] = (value + bq[:, cols]).astype(jnp.bfloat16)
        return carry

    lax.fori_loop(0, parts, project, 0)
    service_first()

    contract = (((1,), (1,)), ((), ()))

    def head(h, carry):
        start = (h * HEAD) // 128 * 128
        lead = h * HEAD - start
        lane = lax.broadcasted_iota(jnp.int32, (1, 256), 1)
        inside = (lane >= lead) & (lane < lead + HEAD)
        q = joint[:, pl.ds(pl.multiple_of(start, 128), 256)]
        k = joint[:, pl.ds(pl.multiple_of(features + start, 128), 256)]
        v = joint[:, pl.ds(pl.multiple_of(2 * features + start, 128), 256)]
        zero = jnp.zeros_like(k)
        k = jnp.where(inside, k, zero)
        v = jnp.where(inside, v, zero)
        scores = lax.dot_general(q, k, contract, preferred_element_type=jnp.float32)
        scores = scores / math.sqrt(HEAD) + maskb[...]
        top = jnp.max(scores, axis=-1, keepdims=True)
        weights_ = jnp.exp(scores - top)
        total = jnp.sum(weights_, axis=-1, keepdims=True)
        soft = (weights_ * (1.0 / total)).astype(jnp.bfloat16)
        mixed = jnp.dot(soft, v, preferred_element_type=jnp.float32)
        into = pl.ds(pl.multiple_of(start, 128), 256)
        att[:, into] = att[:, into] + mixed.astype(jnp.bfloat16)
        return carry

    lax.fori_loop(0, 8, head, 0)
    service_second(0)
    pass_on(4)
    lax.fori_loop(8, 16, head, 0)
    service_across()
    pass_on(4)

    wo_copy.wait()
    for start, width in ((0, 512), (512, 512), (1024, 384)):
        cols = slice(start, start + width)
        value = jnp.dot(att[:, 0:features], wo[:, cols], preferred_element_type=jnp.float32)
        resid[:, cols] = tokens[:, cols].astype(jnp.float32) + value
    norm_rows(lambda at: resid[at, :], write_acts, 1)
    swap = push(acts.at[pl.ds(0, rows_here)], acts.at[pl.ds(rows_here, rows_here)], partner)
    service_second(1)
    pass_on(4)
    acc[...] = jnp.zeros_like(acc)
    swap.wait_recv()

    def ffn(slots):
        def body(t, carry):
            code = jnp.int32(0)
            for n, (i, k) in enumerate(slots):
                code = jnp.where(t == n, jnp.int32(i * 4 + k), code)
            i, k = code // 4, code % 4
            pre = lax.dot_general(acts[...], wa[k, i], contract, preferred_element_type=jnp.float32)
            hidden = (0.5 * pre * (1.0 + lax.erf(pre * math.sqrt(0.5)))).astype(jnp.bfloat16)
            for start, width in ((0, 512), (512, 512), (1024, 384)):
                acc[:, start : start + width] += jnp.dot(
                    hidden, wb[k, i, :, start : start + width], preferred_element_type=jnp.float32
                )
            return carry

        lax.fori_loop(0, len(slots), body, 0)

    done_final = [0]

    def finish_shares():
        pass_on(len(passing))
        arrived(final[done_final[0] :])
        done_final[0] = len(final)

    service_second(3)
    service_last(0)
    pass_on(12)
    service_second(2)
    arrived(final)
    done_final[0] = len(final)
    ffn([(0, 0), (1, 0), (3, 0), (0, 1), (0, 3), (2, 0), (0, 2)])
    service_last(1)
    pass_on(10)
    service_last(3)
    pass_on(2)
    arrived(final[done_final[0] :])
    done_final[0] = len(final)
    ffn([(1, 1), (1, 3), (3, 1), (3, 3)])
    service_last(2)
    finish_shares()
    ffn([(1, 2), (2, 1), (3, 2), (2, 3), (2, 2)])

    def narrow(t, carry):
        at = pl.multiple_of(t * 32, 32)
        psend[pl.ds(at, 32), :] = acc[pl.ds(rows_here + at, 32), :].astype(jnp.bfloat16)
        return carry

    lax.fori_loop(0, rows_here // 32, narrow, 0)
    back = push(psend, precv, partner)
    back.wait_recv()

    def write_att(at, value):
        att[at, 0:features] = value.astype(jnp.bfloat16)

    norm_rows(
        lambda at: resid[at, :] + (acc[at, :] + precv[at, :].astype(jnp.float32)), write_att, 2
    )
    for q in range(4):
        place = lax.broadcasted_iota(jnp.int32, (MERGED_DEV, rows_here), 1)
        pick = (idx[:, q : q + 1] == place).astype(jnp.bfloat16)
        merged_out[:, q * features : (q + 1) * features] = jnp.dot(
            pick, att[:, 0:features], preferred_element_type=jnp.float32
        ).astype(jnp.bfloat16)
    for copy in sent:
        copy.wait_send()


def layer(tokens, gain, bias, wq, bq, wo, wa, wb, seg, idx):
    rows_here, features = tokens.shape
    vmem = pl.BlockSpec(memory_space=pltpu.VMEM)
    hbm = pl.BlockSpec(memory_space=pl.ANY)
    copies = 2 * (2 + 2 + 16) + 90 + 2
    return pl.pallas_call(
        layer_kernel,
        out_shape=jax.ShapeDtypeStruct((MERGED_DEV, 4 * features), jnp.bfloat16),
        in_specs=[vmem, vmem, vmem, hbm, vmem, hbm, hbm, hbm, vmem, vmem],
        out_specs=vmem,
        scratch_shapes=[
            pltpu.VMEM((4, 4, SLOT, features), jnp.bfloat16),
            pltpu.VMEM((4, 4, SLOT, features), jnp.bfloat16),
            pltpu.VMEM((features, 3 * features), jnp.bfloat16),
            pltpu.VMEM((features, features), jnp.bfloat16),
            pltpu.VMEM((rows_here, 3 * features + 128), jnp.bfloat16),
            pltpu.VMEM((2 * rows_here, features), jnp.bfloat16),
            pltpu.VMEM((rows_here, features), jnp.float32),
            pltpu.VMEM((2 * rows_here, features), jnp.float32),
            pltpu.VMEM((rows_here, features + 128), jnp.bfloat16),
            pltpu.VMEM((rows_here, rows_here), jnp.float32),
            pltpu.VMEM((rows_here, features), jnp.bfloat16),
            pltpu.VMEM((rows_here, features), jnp.bfloat16),
            pltpu.SemaphoreType.DMA((copies,)),
            pltpu.SemaphoreType.DMA((copies,)),
            pltpu.SemaphoreType.DMA((22,)),
        ],
        compiler_params=pltpu.CompilerParams(
            collective_id=1, has_side_effects=True, vmem_limit_bytes=60 * 1024 * 1024
        ),
        name="layer",
    )(tokens, gain, bias, wq, bq, wo, wa, wb, seg, idx)


def per_device(
    tokens,
    norm_gain,
    norm_bias,
    input_weight,
    input_bias,
    output_weight,
    expand_weight,
    reduce_weight,
    merger_weight,
    output_gain,
    segments,
    grid_sides,
    routes,
):
    rows_here = tokens.shape[0]
    features = tokens.shape[1]
    n_rows = lax.axis_size("rows")
    n_mlp = lax.axis_size("mlp")
    member = lax.axis_index("mlp")
    own_grid = lax.dynamic_slice_in_dim(grid_sides, member * REQ_DEV, REQ_DEV, 0)
    token_index, is_valid, owner_slot, own_counts = merge_layout(own_grid)
    token_index = jnp.where(is_valid[:, None], token_index, -1)
    merged = layer(
        tokens,
        norm_gain,
        norm_bias,
        input_weight,
        input_bias[None, :],
        output_weight,
        expand_weight,
        reduce_weight,
        segments[None, :],
        token_index,
    )
    projected = jnp.dot(
        lax.all_gather(merged, "mlp", axis=0, tiled=True),
        merger_weight,
        preferred_element_type=jnp.float32,
    )
    group_index, group_valid, group_owner, group_counts = jax.vmap(merge_layout)(
        grid_sides.reshape(n_mlp, REQ_DEV, 2)
    )
    group_requests = n_mlp * REQ_DEV
    member_base = (REQ_DEV * jnp.arange(n_mlp, dtype=jnp.int32))[:, None]
    request_of_row = jnp.where(group_valid, group_owner + member_base, group_requests).reshape(-1)
    counts = group_counts.reshape(-1)
    gained = projected * output_gain
    row_squares = jnp.sum(projected * projected, axis=1)
    row_peaks = jnp.max(gained, axis=1)
    member_of = jnp.arange(group_requests, dtype=jnp.int32)[:, None] == request_of_row[None, :]
    sums_part = jnp.sum(jnp.where(member_of, row_squares[None, :], 0.0), axis=1)
    peaks_part = jnp.max(jnp.where(member_of, row_peaks[None, :], -jnp.inf), axis=1)
    square_sum, peak_all = combined_all((sums_part, peaks_part), "mlp", combine_totals)
    inv_rms = lax.rsqrt(square_sum / (jnp.maximum(counts, 1).astype(jnp.float32) * OUT) + EPS)
    row_inv = jnp.sum(jnp.where(member_of, inv_rms[:, None], 0.0), axis=0)
    scaled = (gained * row_inv[:, None]).astype(jnp.bfloat16)
    peak_values = jnp.where(counts > 0, peak_all * inv_rms, 0.0)
    peaks_own = lax.dynamic_slice_in_dim(peak_values, member * REQ_DEV, REQ_DEV, 0)
    targets = routes[:, 0]
    group_rows = targets.shape[0]
    row_order = jnp.arange(group_rows, dtype=jnp.int32)
    same_target = (targets[:, None] == targets[None, :]) & (row_order[None, :] < row_order[:, None])
    target_rank = jnp.sum(same_target.astype(jnp.int32), axis=1)
    devices = n_rows * n_mlp
    capacity = max(2, 2 * MERGED_DEV // n_rows)
    slot_key = target_rank * devices + targets
    selector = (
        jnp.arange(capacity * devices, dtype=jnp.int32)[:, None] == slot_key[None, :]
    ).astype(jnp.bfloat16)
    outgoing = jnp.dot(selector, scaled, preferred_element_type=jnp.float32).astype(jnp.bfloat16)
    outgoing = outgoing.reshape(capacity, devices, scaled.shape[1])
    arrived = lax.all_to_all(outgoing, ("rows", "mlp"), split_axis=1, concat_axis=2, tiled=True)
    delivered = arrived.reshape(capacity * n_rows, n_mlp * scaled.shape[1])
    return (delivered, peaks_own)


def solution(mesh):
    return jax.shard_map(
        per_device,
        mesh=mesh,
        in_specs=(
            P(("rows", "mlp"), None),
            P(),
            P(),
            P(),
            P(),
            P(),
            P("rows", None),
            P("rows", None),
            P(None, "mlp"),
            P("mlp"),
            P(("rows", "mlp")),
            P("rows", None),
            P("rows", None),
        ),
        out_specs=(P(("rows", "mlp"), None), P(("rows", "mlp"))),
        check_vma=False,
    )
```

```python
import math

import jax
import jax.numpy as jnp
from jax import lax
from jax.experimental import pallas as pl
from jax.experimental.pallas import tpu as pltpu
from jax.sharding import PartitionSpec as P

HEADS = 16
HEAD = 88
OUT = 4096
REQ_DEV = 4
MERGED_DEV = 64


EPS = 1e-06


def merge_layout(grid_block):
    heights = grid_block[:, 0]
    widths_all = grid_block[:, 1]
    lengths = jnp.where(heights > 0, 1 + heights * widths_all, 0)
    starts = jnp.cumsum(lengths) - lengths
    counts = heights // 2 * (widths_all // 2)
    merge_starts = jnp.cumsum(counts) - counts
    merge_ends = merge_starts + counts
    merge_slots = jnp.arange(MERGED_DEV, dtype=jnp.int32)
    owner_slot = jnp.sum((merge_ends[None, :] <= merge_slots[:, None]).astype(jnp.int32), axis=1)
    is_valid = owner_slot < REQ_DEV
    chosen = (owner_slot[:, None] == jnp.arange(REQ_DEV, dtype=jnp.int32)[None, :]).astype(
        jnp.int32
    )
    row_width = jnp.sum(chosen * widths_all[None, :], axis=1)
    row_start = jnp.sum(chosen * starts[None, :], axis=1)
    row_merge = jnp.sum(chosen * merge_starts[None, :], axis=1)
    within = merge_slots - row_merge
    half_width = jnp.maximum(row_width // 2, 1)
    patch_row = within // half_width
    patch_col = within - patch_row * half_width
    corner = row_start + 1 + 2 * patch_row * row_width + 2 * patch_col
    token_index = jnp.stack(
        [corner, corner + 1, corner + row_width, corner + row_width + 1], axis=1
    )
    token_index = jnp.where(is_valid[:, None], token_index, 0)
    return (token_index, is_valid, owner_slot, counts)


MESH = pl.DeviceIdType.MESH
PLANE = 144
HALF = 80
SHARE = 16
SLOT = 192


def layer_kernel(
    tokens, gain, bias, wq_hbm, bq, wo_hbm, wa_hbm, wb_hbm, seg, idx, merged_out,
    wa, wb, wq, wo, joint, acts, resid, acc, att, maskb, psend, precv,
    send, recv, local,
):
    row = lax.axis_index("rows")
    member = lax.axis_index("mlp")
    x, z = row // 4, row % 4
    y, core = member // 2, member % 2
    features = tokens.shape[1]
    rows_here = tokens.shape[0]

    def plane(dx, dz):
        return (((x + dx + 4) % 4) * 4 + (z + dz + 4) % 4, member)

    def column(dy):
        return (row, ((y + dy + 4) % 4) * 2 + core)

    partner = (row, member + 1 - 2 * core)
    near = [plane(1, 0), plane(-1, 0), plane(0, 1), plane(0, -1), column(1), column(-1), partner]

    started = []

    def load(src, dst):
        copy = pltpu.make_async_copy(src, dst, local.at[len(started)])
        copy.start()
        started.append(copy)
        return copy

    own = []
    first = SLOT - 4 * SHARE
    for hbm, vmem in ((wa_hbm, wa), (wb_hbm, wb)):
        base = pl.multiple_of(core * SLOT, 16)
        own.append(load(hbm.at[pl.ds(base, first)], vmem.at[0, 0, pl.ds(0, first)]))
        for place, offset in enumerate((0, -1, 1, 2)):
            at = pl.multiple_of(core * SLOT + first + SHARE * ((y + offset + 4) % 4), 16)
            own.append(
                load(hbm.at[pl.ds(at, SHARE)], vmem.at[0, 0, pl.ds(first + place * SHARE, SHARE)])
            )
    chunk = 384
    parts = wq_hbm.shape[1] // chunk
    first_wq = len(started)
    for j in range(parts):
        load(wq_hbm.at[:, pl.ds(j * chunk, chunk)], wq.at[:, pl.ds(j * chunk, chunk)])
    wo_copy = load(wo_hbm, wo)

    barrier = pltpu.get_barrier_semaphore()
    for device in near:
        pl.semaphore_signal(barrier, inc=1, device_id=device, device_id_type=MESH)
    pl.semaphore_wait(barrier, len(near))

    sent = []

    def push(src, dst, device):
        k = len(sent)
        copy = pltpu.make_async_remote_copy(
            src_ref=src, dst_ref=dst, send_sem=send.at[k], recv_sem=recv.at[k],
            device_id=device, device_id_type=MESH,
        )
        copy.start()
        sent.append(copy)
        return copy

    def slot_a(i, k):
        return wa.at[k, i]

    def slot_b(i, k):
        return wb.at[i, k]

    def step_x(s):
        return plane(s, 0)

    def step_z(s):
        return plane(0, s)

    weights = ((slot_a, step_x, step_z), (slot_b, step_z, step_x))
    up, low, whole = pl.ds(0, HALF), pl.ds(HALF, PLANE - HALF), pl.ds(0, PLANE)

    def send_first(w):
        slot, one, _ = w
        return [
            push(slot(0, 0).at[whole], slot(3, 0).at[whole], one(1)),
            push(slot(0, 0).at[whole], slot(1, 0).at[whole], one(-1)),
        ]

    def forward_first(w):
        slot, one, _ = w
        return [
            push(slot(3, 0).at[up], slot(2, 0).at[up], one(1)),
            push(slot(1, 0).at[low], slot(2, 0).at[low], one(-1)),
        ]

    def send_second(w, i):
        slot, _, two = w
        return [
            push(slot(i, 0).at[whole], slot(i, 3).at[whole], two(1)),
            push(slot(i, 0).at[whole], slot(i, 1).at[whole], two(-1)),
        ]

    def forward_second(w, i):
        slot, _, two = w
        return [
            push(slot(i, 3).at[up], slot(i, 2).at[up], two(1)),
            push(slot(i, 1).at[low], slot(i, 2).at[low], two(-1)),
        ]

    share = [pl.ds(first + j * SHARE, SHARE) for j in range(4)]

    def share_out(w, i, k):
        slot = w[0]
        return [
            push(slot(i, k).at[share[0]], slot(i, k).at[share[1]], column(1)),
            push(slot(i, k).at[share[0]], slot(i, k).at[share[2]], column(-1)),
        ]

    def share_on(w, i, k):
        slot = w[0]
        if (i + k) % 2 == 0:
            return push(slot(i, k).at[share[1]], slot(i, k).at[share[3]], column(1))
        return push(slot(i, k).at[share[2]], slot(i, k).at[share[3]], column(-1))

    def arrived(copies):
        for copy in copies:
            copy.wait_recv()

    for copy in own:
        copy.wait()
    table = {}
    for n, w in enumerate(weights):
        table["s1", n] = send_first(w)
    for n, w in enumerate(weights):
        table["s2", n, 0] = send_second(w, 0)

    passing = []

    def spread(slots):
        for n, i, k in slots:
            passing.append((n, i, k, share_out(weights[n], i, k)))

    final = []

    def pass_on(count):
        for _ in range(min(count, len(passing))):
            n, i, k, copies = passing.pop(0)
            arrived(copies)
            final.append(share_on(weights[n], i, k))

    def service_first():
        for n in (0, 1):
            arrived(table["s1", n])
        for n in (0, 1):
            table["f1", n] = forward_first(weights[n])
        for n in (0, 1):
            for i in (1, 3):
                table["s2", n, i] = send_second(weights[n], i)
        spread([(n, i, 0) for n in (0, 1) for i in (1, 3)])

    def service_second(i):
        for n in (0, 1):
            arrived(table["s2", n, i])
            table["f2", n, i] = forward_second(weights[n], i)
        spread([(n, i, k) for n in (0, 1) for k in (1, 3)])

    def service_across():
        for n in (0, 1):
            arrived(table["f1", n])
            table["s2", n, 2] = send_second(weights[n], 2)
        spread([(n, 2, 0) for n in (0, 1)])

    def service_last(i):
        for n in (0, 1):
            arrived(table["f2", n, i])
        spread([(n, i, 2) for n in (0, 1)])

    def norm_rows(read, write, i):
        def body(t, carry):
            at = pl.ds(pl.multiple_of(t * 32, 32), 32)
            value = read(at)
            mean = jnp.mean(value, axis=-1, keepdims=True)
            centered = value - mean
            variance = jnp.mean(centered * centered, axis=-1, keepdims=True)
            write(at, centered * lax.rsqrt(variance + EPS) * gain[i : i + 1, :] + bias[i : i + 1, :])
            return carry

        lax.fori_loop(0, rows_here // 32, body, 0)

    def write_acts(at, value):
        acts[at, :] = value.astype(jnp.bfloat16)

    norm_rows(lambda at: tokens[at, :].astype(jnp.float32), write_acts, 0)
    seg_f = jnp.broadcast_to(seg[...].astype(jnp.float32), (rows_here, rows_here))
    maskb[...] = jnp.where(seg_f == seg_f.T, 0.0, -jnp.inf)
    joint[:, parts * chunk :] = jnp.zeros((rows_here, joint.shape[1] - parts * chunk), jnp.bfloat16)
    att[...] = jnp.zeros_like(att)

    def project(j, carry):
        cols = pl.ds(pl.multiple_of(j * chunk, chunk), chunk)
        pltpu.make_async_copy(wq_hbm.at[:, cols], wq.at[:, cols], local.at[first_wq + j]).wait()
        value = jnp.dot(acts[0:rows_here, :], wq[:, cols], preferred_element_type=jnp.float32)
        joint[:, cols] = (value + bq[:, cols]).astype(jnp.bfloat16)
        return carry

    lax.fori_loop(0, parts, project, 0)
    service_first()

    contract = (((1,), (1,)), ((), ()))

    def head(h, carry):
        start = (h * HEAD) // 128 * 128
        lead = h * HEAD - start
        lane = lax.broadcasted_iota(jnp.int32, (1, 256), 1)
        inside = (lane >= lead) & (lane < lead + HEAD)
        q = joint[:, pl.ds(pl.multiple_of(start, 128), 256)]
        k = joint[:, pl.ds(pl.multiple_of(features + start, 128), 256)]
        v = joint[:, pl.ds(pl.multiple_of(2 * features + start, 128), 256)]
        zero = jnp.zeros_like(k)
        k = jnp.where(inside, k, zero)
        v = jnp.where(inside, v, zero)
        scores = lax.dot_general(q, k, contract, preferred_element_type=jnp.float32)
        scores = scores / math.sqrt(HEAD) + maskb[...]
        top = jnp.max(scores, axis=-1, keepdims=True)
        weights_ = jnp.exp(scores - top)
        total = jnp.sum(weights_, axis=-1, keepdims=True)
        soft = (weights_ * (1.0 / total)).astype(jnp.bfloat16)
        mixed = jnp.dot(soft, v, preferred_element_type=jnp.float32)
        into = pl.ds(pl.multiple_of(start, 128), 256)
        att[:, into] = att[:, into] + mixed.astype(jnp.bfloat16)
        return carry

    lax.fori_loop(0, 8, head, 0)
    service_second(0)
    pass_on(4)
    lax.fori_loop(8, 16, head, 0)
    service_across()
    pass_on(4)

    wo_copy.wait()
    for start, width in ((0, 512), (512, 512), (1024, 384)):
        cols = slice(start, start + width)
        value = jnp.dot(att[:, 0:features], wo[:, cols], preferred_element_type=jnp.float32)
        resid[:, cols] = tokens[:, cols].astype(jnp.float32) + value
    norm_rows(lambda at: resid[at, :], write_acts, 1)
    swap = push(acts.at[pl.ds(0, rows_here)], acts.at[pl.ds(rows_here, rows_here)], partner)
    service_second(1)
    pass_on(4)
    acc[...] = jnp.zeros_like(acc)
    swap.wait_recv()

    def ffn(slots):
        def body(t, carry):
            code = jnp.int32(0)
            for n, (i, k) in enumerate(slots):
                code = jnp.where(t == n, jnp.int32(i * 4 + k), code)
            i, k = code // 4, code % 4
            pre = lax.dot_general(acts[...], wa[k, i], contract, preferred_element_type=jnp.float32)
            hidden = (0.5 * pre * (1.0 + lax.erf(pre * math.sqrt(0.5)))).astype(jnp.bfloat16)
            for start, width in ((0, 512), (512, 512), (1024, 384)):
                acc[:, start : start + width] += jnp.dot(
                    hidden, wb[k, i, :, start : start + width], preferred_element_type=jnp.float32
                )
            return carry

        lax.fori_loop(0, len(slots), body, 0)

    done_final = [0]

    def finish_shares():
        pass_on(len(passing))
        arrived(final[done_final[0] :])
        done_final[0] = len(final)

    service_second(3)
    service_last(0)
    pass_on(12)
    service_second(2)
    arrived(final)
    done_final[0] = len(final)
    ffn([(0, 0), (1, 0), (3, 0), (0, 1), (0, 3), (2, 0), (0, 2)])
    service_last(1)
    pass_on(10)
    service_last(3)
    pass_on(2)
    arrived(final[done_final[0] :])
    done_final[0] = len(final)
    ffn([(1, 1), (1, 3), (3, 1), (3, 3)])
    service_last(2)
    finish_shares()
    ffn([(1, 2), (2, 1), (3, 2), (2, 3), (2, 2)])

    def narrow(t, carry):
        at = pl.multiple_of(t * 32, 32)
        psend[pl.ds(at, 32), :] = acc[pl.ds(rows_here + at, 32), :].astype(jnp.bfloat16)
        return carry

    lax.fori_loop(0, rows_here // 32, narrow, 0)
    back = push(psend, precv, partner)
    back.wait_recv()

    def write_att(at, value):
        att[at, 0:features] = value.astype(jnp.bfloat16)

    norm_rows(
        lambda at: resid[at, :] + (acc[at, :] + precv[at, :].astype(jnp.float32)), write_att, 2
    )
    for q in range(4):
        place = lax.broadcasted_iota(jnp.int32, (MERGED_DEV, rows_here), 1)
        pick = (idx[:, q : q + 1] == place).astype(jnp.bfloat16)
        merged_out[:, q * features : (q + 1) * features] = jnp.dot(
            pick, att[:, 0:features], preferred_element_type=jnp.float32
        ).astype(jnp.bfloat16)
    for copy in sent:
        copy.wait_send()


def layer(tokens, gain, bias, wq, bq, wo, wa, wb, seg, idx):
    rows_here, features = tokens.shape
    vmem = pl.BlockSpec(memory_space=pltpu.VMEM)
    hbm = pl.BlockSpec(memory_space=pl.ANY)
    copies = 2 * (2 + 2 + 16) + 90 + 2
    return pl.pallas_call(
        layer_kernel,
        out_shape=jax.ShapeDtypeStruct((MERGED_DEV, 4 * features), jnp.bfloat16),
        in_specs=[vmem, vmem, vmem, hbm, vmem, hbm, hbm, hbm, vmem, vmem],
        out_specs=vmem,
        scratch_shapes=[
            pltpu.VMEM((4, 4, SLOT, features), jnp.bfloat16),
            pltpu.VMEM((4, 4, SLOT, features), jnp.bfloat16),
            pltpu.VMEM((features, 3 * features), jnp.bfloat16),
            pltpu.VMEM((features, features), jnp.bfloat16),
            pltpu.VMEM((rows_here, 3 * features + 128), jnp.bfloat16),
            pltpu.VMEM((2 * rows_here, features), jnp.bfloat16),
            pltpu.VMEM((rows_here, features), jnp.float32),
            pltpu.VMEM((2 * rows_here, features), jnp.float32),
            pltpu.VMEM((rows_here, features + 128), jnp.bfloat16),
            pltpu.VMEM((rows_here, rows_here), jnp.float32),
            pltpu.VMEM((rows_here, features), jnp.bfloat16),
            pltpu.VMEM((rows_here, features), jnp.bfloat16),
            pltpu.SemaphoreType.DMA((copies,)),
            pltpu.SemaphoreType.DMA((copies,)),
            pltpu.SemaphoreType.DMA((22,)),
        ],
        compiler_params=pltpu.CompilerParams(
            collective_id=1, has_side_effects=True, vmem_limit_bytes=60 * 1024 * 1024
        ),
        name="layer",
    )(tokens, gain, bias, wq, bq, wo, wa, wb, seg, idx)


def merger_kernel(
    merged, w_hbm, gain, req, counts, routes, outgoing, peaks,
    blocks, weight, acc, scaled, stats, gathered, send, recv, local,
):
    row = lax.axis_index("rows")
    member = lax.axis_index("mlp")
    y, core = member // 2, member % 2
    parts = 4
    depth = w_hbm.shape[0] // parts
    group = 8 * MERGED_DEV

    def at_y(dy, other=False):
        side = 1 - core if other else core
        return ((y + dy + 4) % 4) * 2 + side

    started = []
    for q in range(parts):
        copy = pltpu.make_async_copy(
            merged.at[:, pl.ds(q * depth, depth)], blocks.at[q, member], local.at[q]
        )
        copy.start()
        started.append(copy)
    fetched = []
    for q in range(parts):
        rows_q = pl.ds(q * depth, depth)
        copy = pltpu.make_async_copy(w_hbm.at[rows_q], weight.at[rows_q], local.at[parts + q])
        copy.start()
        fetched.append(copy)

    barrier = pltpu.get_barrier_semaphore()
    for step in range(1, 8):
        pl.semaphore_signal(
            barrier, inc=1, device_id=(row, (member + step) % 8), device_id_type=MESH
        )
    pl.semaphore_wait(barrier, 7)

    sent = []

    def push(src, dst, to):
        k = len(sent)
        copy = pltpu.make_async_remote_copy(
            src_ref=src, dst_ref=dst, send_sem=send.at[k], recv_sem=recv.at[k],
            device_id=(row, to), device_id_type=MESH,
        )
        copy.start()
        sent.append(copy)
        return copy

    half = MERGED_DEV // 2
    up, low = pl.ds(0, half), pl.ds(half, half)
    first = []
    for q in range(parts):
        started[q].wait()
        mine = blocks.at[q, member]
        first.append([push(mine, mine, at_y(1)), push(mine, mine, at_y(-1))])
    swap = []
    for q in range(parts):
        mine = blocks.at[q, member]
        swap.append([push(mine, mine, at_y(0, True))])

    wide = jnp.broadcast_to(routes[...].astype(jnp.float32), (group, 128))
    target_row = wide.T[0:1, :].astype(jnp.int32)
    rank = jnp.zeros((1, group), jnp.int32)
    for t in range(4):
        here = lax.broadcasted_iota(jnp.int32, (128, group), 0) + 128 * t
        there = lax.broadcasted_iota(jnp.int32, (128, group), 1)
        same = (routes[128 * t : 128 * (t + 1), :] == target_row) & (here < there)
        rank = rank + jnp.sum(jnp.where(same, 1, 0), axis=0, keepdims=True)
    key = target_row * 8 + rank

    across = []
    for q in range(parts + 1):
        if q < parts:
            below = blocks.at[q, at_y(-1)]
            above = blocks.at[q, at_y(1)]
            first[q][0].wait_recv()
            across_q = [push(below.at[up], below.at[up], at_y(1))]
            swap[q].append(push(below, below, at_y(0, True)))
            first[q][1].wait_recv()
            across_q.append(push(above.at[low], above.at[low], at_y(-1)))
            swap[q].append(push(above, above, at_y(0, True)))
            across.append(across_q)
        if q >= 1:
            p = q - 1
            far = blocks.at[p, at_y(2)]
            across[p][0].wait_recv()
            across[p][1].wait_recv()
            swap[p].append(push(far, far, at_y(0, True)))
            fetched[p].wait()
            for copy in swap[p]:
                copy.wait_recv()

            def column(n, carry, p=p):
                cols = pl.ds(pl.multiple_of(n * 256, 256), 256)
                value = jnp.dot(
                    blocks[p].reshape(group, depth),
                    weight[p * depth : (p + 1) * depth, cols],
                    preferred_element_type=jnp.float32,
                )
                if p == 0:
                    acc[:, cols] = value
                else:
                    acc[:, cols] += value
                return carry

            lax.fori_loop(0, acc.shape[1] // 256, column, 0)

    lane = lax.broadcasted_iota(jnp.int32, (MERGED_DEV, 128), 1)

    def tally(t, carry):
        sums, tops = carry
        at = pl.ds(pl.multiple_of(t * MERGED_DEV, MERGED_DEV), MERGED_DEV)
        value = acc[at, :]
        squares = jnp.sum(value * value, axis=1, keepdims=True)
        top = jnp.max(value * gain[...], axis=1, keepdims=True)
        owns = req[at, :] == lane
        sums = sums + jnp.sum(jnp.where(owns, squares, 0.0), axis=0, keepdims=True)
        tops = jnp.maximum(tops, jnp.max(jnp.where(owns, top, -jnp.inf), axis=0, keepdims=True))
        return sums, tops

    sums, tops = lax.fori_loop(
        0, 8, tally, (jnp.zeros((1, 128), jnp.float32), jnp.full((1, 128), -jnp.inf, jnp.float32))
    )
    place = lax.broadcasted_iota(jnp.int32, (8, 128), 0)
    both = jnp.where(place == 0, sums, tops)
    stats[...] = both
    gathered[member] = both
    told = [push(stats, gathered.at[member], (member + step) % 8) for step in range(1, 8)]
    for copy in told:
        copy.wait_recv()
    total = gathered[0, 0:1, :]
    top = gathered[0, 1:2, :]
    for m in range(1, 8):
        total = total + gathered[m, 0:1, :]
        top = jnp.maximum(top, gathered[m, 1:2, :])
    number = counts[...]
    inv_rms = lax.rsqrt(total / (jnp.maximum(number, 1.0) * OUT) + EPS)
    peaks[...] = jnp.where(number > 0.0, top * inv_rms, 0.0)

    def scale(t, carry):
        at = pl.ds(pl.multiple_of(t * MERGED_DEV, MERGED_DEV), MERGED_DEV)
        row_inv = jnp.sum(jnp.where(req[at, :] == lane, inv_rms, 0.0), axis=1, keepdims=True)
        scaled[at, :] = (acc[at, :] * gain[...] * row_inv).astype(jnp.bfloat16)
        return carry

    lax.fori_loop(0, 8, scale, 0)

    def route(t, carry):
        at = pl.multiple_of(t * 256, 256)
        slot = lax.broadcasted_iota(jnp.int32, (256, group), 0) + at
        pick = (slot == key).astype(jnp.bfloat16)
        outgoing[pl.ds(at, 256), :] = jnp.dot(
            pick, scaled[...], preferred_element_type=jnp.float32
        ).astype(jnp.bfloat16)
        return carry

    lax.fori_loop(0, outgoing.shape[0] // 256, route, 0)
    for copy in sent:
        copy.wait_send()


def merger(merged, weight, gain, req, counts, routes):
    vmem = pl.BlockSpec(memory_space=pltpu.VMEM)
    hbm = pl.BlockSpec(memory_space=pl.ANY)
    depth, width = weight.shape
    group = 8 * MERGED_DEV
    copies = 32 + 7
    return pl.pallas_call(
        merger_kernel,
        out_shape=(
            jax.ShapeDtypeStruct((1024, width), jnp.bfloat16),
            jax.ShapeDtypeStruct((1, 128), jnp.float32),
        ),
        in_specs=[hbm, hbm, vmem, vmem, vmem, vmem],
        out_specs=(vmem, vmem),
        scratch_shapes=[
            pltpu.VMEM((4, 8, MERGED_DEV, depth // 4), jnp.bfloat16),
            pltpu.VMEM((depth, width), jnp.bfloat16),
            pltpu.VMEM((group, width), jnp.float32),
            pltpu.VMEM((group, width), jnp.bfloat16),
            pltpu.VMEM((8, 128), jnp.float32),
            pltpu.VMEM((8, 8, 128), jnp.float32),
            pltpu.SemaphoreType.DMA((copies,)),
            pltpu.SemaphoreType.DMA((copies,)),
            pltpu.SemaphoreType.DMA((8,)),
        ],
        compiler_params=pltpu.CompilerParams(
            collective_id=2, has_side_effects=True, vmem_limit_bytes=60 * 1024 * 1024
        ),
        name="merger",
    )(merged, weight, gain, req, counts, routes)


def per_device(
    tokens,
    norm_gain,
    norm_bias,
    input_weight,
    input_bias,
    output_weight,
    expand_weight,
    reduce_weight,
    merger_weight,
    output_gain,
    segments,
    grid_sides,
    routes,
):
    n_rows = lax.axis_size("rows")
    n_mlp = lax.axis_size("mlp")
    member = lax.axis_index("mlp")
    own_grid = lax.dynamic_slice_in_dim(grid_sides, member * REQ_DEV, REQ_DEV, 0)
    token_index, is_valid, owner_slot, own_counts = merge_layout(own_grid)
    token_index = jnp.where(is_valid[:, None], token_index, -1)
    merged = layer(
        tokens,
        norm_gain,
        norm_bias,
        input_weight,
        input_bias[None, :],
        output_weight,
        expand_weight,
        reduce_weight,
        segments[None, :],
        token_index,
    )
    group_valid, group_owner, group_counts = jax.vmap(merge_layout)(
        grid_sides.reshape(n_mlp, REQ_DEV, 2)
    )[1:]
    group_requests = n_mlp * REQ_DEV
    member_base = (REQ_DEV * jnp.arange(n_mlp, dtype=jnp.int32))[:, None]
    request_of_row = jnp.where(group_valid, group_owner + member_base, 128).reshape(-1, 1)
    counts = jnp.pad(group_counts.reshape(1, -1).astype(jnp.float32), ((0, 0), (0, 128 - group_requests)))
    outgoing, peak_values = merger(
        merged, merger_weight, output_gain[None, :], request_of_row, counts, routes
    )
    peaks_own = lax.dynamic_slice_in_dim(peak_values[0], member * REQ_DEV, REQ_DEV, 0)
    capacity = outgoing.shape[0] // (n_rows * n_mlp)
    outgoing = outgoing.reshape(n_rows * n_mlp, capacity, -1)
    arrived = lax.all_to_all(outgoing, ("rows", "mlp"), split_axis=0, concat_axis=0, tiled=True)
    arrived = arrived.reshape(n_rows, n_mlp, capacity, -1)
    delivered = arrived.transpose(2, 0, 1, 3).reshape(capacity * n_rows, -1)
    return (delivered, peaks_own)


def solution(mesh):
    return jax.shard_map(
        per_device,
        mesh=mesh,
        in_specs=(
            P(("rows", "mlp"), None),
            P(),
            P(),
            P(),
            P(),
            P(),
            P("rows", None),
            P("rows", None),
            P(None, "mlp"),
            P("mlp"),
            P(("rows", "mlp")),
            P("rows", None),
            P("rows", None),
        ),
        out_specs=(P(("rows", "mlp"), None), P(("rows", "mlp"))),
        check_vma=False,
    )
```

```python
import math

import jax
import jax.numpy as jnp
from jax import lax
from jax.experimental import pallas as pl
from jax.experimental.pallas import tpu as pltpu
from jax.sharding import PartitionSpec as P

HEADS = 16
HEAD = 88
OUT = 4096
REQ_DEV = 4
MERGED_DEV = 64


EPS = 1e-06


MESH = pl.DeviceIdType.MESH


def request_spans(grid, first):
    spans = []
    token, merge = 0, 0
    for k in range(REQ_DEV):
        height, width = grid[first + k, 0], grid[first + k, 1]
        count = lax.div(height, 2) * lax.div(width, 2)
        spans.append((height, width, token, merge, count))
        token = token + jnp.where(height > 0, 1 + height * width, 0)
        merge = merge + count
    return spans


PLANE = 144
HALF = 80
SHARE = 16
SLOT = 192


def layer_kernel(
    tokens, gain, bias, wq_hbm, bq, wo_hbm, wa_hbm, wb_hbm, seg, grid, merged_out,
    wa, wb, wq, wo, joint, acts, resid, acc, att, maskb, pick, psend, precv,
    send, recv, local,
):
    row = lax.axis_index("rows")
    member = lax.axis_index("mlp")
    x, z = row // 4, row % 4
    y, core = member // 2, member % 2
    zero = row - row
    features = tokens.shape[1]
    rows_here = tokens.shape[0]

    def plane(dx, dz):
        return (((x + dx + 4) % 4) * 4 + (z + dz + 4) % 4, member)

    def column(dy):
        return (row, ((y + dy + 4) % 4) * 2 + core)

    partner = (row, member + 1 - 2 * core)
    near = [plane(1, 0), plane(-1, 0), plane(0, 1), plane(0, -1), column(1), column(-1), partner]

    started = []

    def load(src, dst):
        copy = pltpu.make_async_copy(src, dst, local.at[len(started)])
        copy.start()
        started.append(copy)
        return copy

    own = []
    first = SLOT - 4 * SHARE
    for hbm, vmem in ((wa_hbm, wa), (wb_hbm, wb)):
        base = pl.multiple_of(core * SLOT, 16)
        own.append(load(hbm.at[pl.ds(base, first)], vmem.at[0, 0, pl.ds(0, first)]))
        for place, offset in enumerate((0, -1, 1, 2)):
            at = pl.multiple_of(core * SLOT + first + SHARE * ((y + offset + 4) % 4), 16)
            own.append(
                load(hbm.at[pl.ds(at, SHARE)], vmem.at[0, 0, pl.ds(first + place * SHARE, SHARE)])
            )
    chunk = 384
    parts = wq_hbm.shape[1] // chunk
    first_wq = len(started)
    for j in range(parts):
        load(wq_hbm.at[:, pl.ds(j * chunk, chunk)], wq.at[:, pl.ds(j * chunk, chunk)])
    wo_copy = load(wo_hbm, wo)

    barrier = pltpu.get_barrier_semaphore()
    for device in near:
        pl.semaphore_signal(barrier, inc=1, device_id=device, device_id_type=MESH)
    pl.semaphore_wait(barrier, len(near))

    sent = []

    def push(src, dst, device):
        k = len(sent)
        copy = pltpu.make_async_remote_copy(
            src_ref=src, dst_ref=dst, send_sem=send.at[k], recv_sem=recv.at[k],
            device_id=device, device_id_type=MESH,
        )
        copy.start()
        sent.append(copy)
        return copy

    def slot_a(i, k):
        return wa.at[k, i]

    def slot_b(i, k):
        return wb.at[i, k]

    def step_x(s):
        return plane(s, 0)

    def step_z(s):
        return plane(0, s)

    weights = ((slot_a, step_x, step_z), (slot_b, step_z, step_x))
    up, low, whole = pl.ds(0, HALF), pl.ds(HALF, PLANE - HALF), pl.ds(0, PLANE)

    def send_first(w):
        slot, one, _ = w
        return [
            push(slot(0, 0).at[whole], slot(3, 0).at[whole], one(1)),
            push(slot(0, 0).at[whole], slot(1, 0).at[whole], one(-1)),
        ]

    def forward_first(w):
        slot, one, _ = w
        return [
            push(slot(3, 0).at[up], slot(2, 0).at[up], one(1)),
            push(slot(1, 0).at[low], slot(2, 0).at[low], one(-1)),
        ]

    def send_second(w, i):
        slot, _, two = w
        return [
            push(slot(i, 0).at[whole], slot(i, 3).at[whole], two(1)),
            push(slot(i, 0).at[whole], slot(i, 1).at[whole], two(-1)),
        ]

    def forward_second(w, i):
        slot, _, two = w
        return [
            push(slot(i, 3).at[up], slot(i, 2).at[up], two(1)),
            push(slot(i, 1).at[low], slot(i, 2).at[low], two(-1)),
        ]

    share = [pl.ds(first + j * SHARE, SHARE) for j in range(4)]

    def share_out(w, i, k):
        slot = w[0]
        return [
            push(slot(i, k).at[share[0]], slot(i, k).at[share[1]], column(1)),
            push(slot(i, k).at[share[0]], slot(i, k).at[share[2]], column(-1)),
        ]

    def share_on(w, i, k):
        slot = w[0]
        if (i + k) % 2 == 0:
            return push(slot(i, k).at[share[1]], slot(i, k).at[share[3]], column(1))
        return push(slot(i, k).at[share[2]], slot(i, k).at[share[3]], column(-1))

    def arrived(copies):
        for copy in copies:
            copy.wait_recv()

    for copy in own:
        copy.wait()
    table = {}
    for n, w in enumerate(weights):
        table["s1", n] = send_first(w)
    for n, w in enumerate(weights):
        table["s2", n, 0] = send_second(w, 0)

    passing = []

    def spread(slots):
        for n, i, k in slots:
            passing.append((n, i, k, share_out(weights[n], i, k)))

    final = []

    def pass_on(count):
        for _ in range(min(count, len(passing))):
            n, i, k, copies = passing.pop(0)
            arrived(copies)
            final.append(share_on(weights[n], i, k))

    def service_first():
        for n in (0, 1):
            arrived(table["s1", n])
        for n in (0, 1):
            table["f1", n] = forward_first(weights[n])
        for n in (0, 1):
            for i in (1, 3):
                table["s2", n, i] = send_second(weights[n], i)
        spread([(n, i, 0) for n in (0, 1) for i in (1, 3)])

    def service_second(i):
        for n in (0, 1):
            arrived(table["s2", n, i])
            table["f2", n, i] = forward_second(weights[n], i)
        spread([(n, i, k) for n in (0, 1) for k in (1, 3)])

    def service_across():
        for n in (0, 1):
            arrived(table["f1", n])
            table["s2", n, 2] = send_second(weights[n], 2)
        spread([(n, 2, 0) for n in (0, 1)])

    def service_last(i):
        for n in (0, 1):
            arrived(table["f2", n, i])
        spread([(n, i, 2) for n in (0, 1)])

    def norm_rows(read, write, i):
        def body(t, carry):
            at = pl.ds(pl.multiple_of(t * 32, 32), 32)
            value = read(at)
            mean = jnp.mean(value, axis=-1, keepdims=True)
            centered = value - mean
            variance = jnp.mean(centered * centered, axis=-1, keepdims=True)
            write(at, centered * lax.rsqrt(variance + EPS) * gain[i : i + 1, :] + bias[i : i + 1, :])
            return carry

        lax.fori_loop(0, rows_here // 32, body, 0, unroll=2)

    def write_acts(at, value):
        acts[at, :] = value.astype(jnp.bfloat16)

    norm_rows(lambda at: tokens[at, :].astype(jnp.float32), write_acts, 0)
    seg_f = jnp.broadcast_to(
        seg[...].astype(jnp.float32).reshape(1, rows_here), (rows_here, rows_here)
    )
    maskb[...] = jnp.where(seg_f == seg_f.T, 0.0, -jnp.inf)
    joint[:, parts * chunk :] = jnp.zeros((rows_here, joint.shape[1] - parts * chunk), jnp.bfloat16)
    att[...] = jnp.zeros_like(att)

    def pick_rows():
        slot = lax.broadcasted_iota(jnp.int32, (MERGED_DEV, rows_here), 0)
        place = lax.broadcasted_iota(jnp.int32, (MERGED_DEV, rows_here), 1)
        corner = jnp.full((MERGED_DEV, rows_here), -1000, jnp.int32)
        wide = jnp.zeros((MERGED_DEV, rows_here), jnp.int32)
        for _, width, token, merge, count in request_spans(grid, member * REQ_DEV):
            within = slot - merge
            half = lax.div(width, 2)
            line = jnp.zeros_like(within)
            for n in range(1, 4):
                line = line + jnp.where(within >= n * half, 1, 0)
            at = token + 1 + 2 * line * width + 2 * (within - line * half)
            here = (within >= 0) & (within < count)
            corner = jnp.where(here, at, corner)
            wide = jnp.where(here, width, wide)
        one, none = jnp.ones((), jnp.float32), jnp.zeros((), jnp.float32)
        for q in range(4):
            at = corner + (q % 2) + (wide if q >= 2 else 0)
            pick[q] = jnp.where(at == place, one, none).astype(jnp.bfloat16)

    def project(j, carry):
        cols = pl.ds(pl.multiple_of(j * chunk, chunk), chunk)
        pltpu.make_async_copy(wq_hbm.at[:, cols], wq.at[:, cols], local.at[first_wq + j]).wait()
        value = jnp.dot(acts[0:rows_here, :], wq[:, cols], preferred_element_type=jnp.float32)
        joint[:, cols] = (value + bq[cols].reshape(1, chunk)).astype(jnp.bfloat16)
        return carry

    lax.fori_loop(0, parts, project, 0)
    service_first()
    pick_rows()

    contract = (((1,), (1,)), ((), ()))

    def head(h, carry):
        start = (h * HEAD) // 128 * 128
        lead = h * HEAD - start
        lane = lax.broadcasted_iota(jnp.int32, (1, 256), 1)
        inside = (lane >= lead) & (lane < lead + HEAD)
        q = joint[:, pl.ds(pl.multiple_of(start, 128), 256)]
        k = joint[:, pl.ds(pl.multiple_of(features + start, 128), 256)]
        v = joint[:, pl.ds(pl.multiple_of(2 * features + start, 128), 256)]
        zero = jnp.zeros_like(k)
        k = jnp.where(inside, k, zero)
        v = jnp.where(inside, v, zero)
        scores = lax.dot_general(q, k, contract, preferred_element_type=jnp.float32)
        scores = scores / math.sqrt(HEAD) + maskb[...]
        top = jnp.max(scores, axis=-1, keepdims=True)
        weights_ = jnp.exp(scores - top)
        total = jnp.sum(weights_, axis=-1, keepdims=True)
        soft = (weights_ * (1.0 / total)).astype(jnp.bfloat16)
        mixed = jnp.dot(soft, v, preferred_element_type=jnp.float32)
        into = pl.ds(pl.multiple_of(start, 128), 256)
        att[:, into] = att[:, into] + mixed.astype(jnp.bfloat16)
        return carry

    lax.fori_loop(0, 6, head, 0, unroll=2)
    pass_on(4)
    lax.fori_loop(6, 10, head, 0, unroll=2)
    service_second(0)
    lax.fori_loop(10, 16, head, 0, unroll=2)
    service_across()
    pass_on(4)

    wo_copy.wait()
    for start, width in ((0, 512), (512, 512), (1024, 384)):
        cols = slice(start, start + width)
        value = jnp.dot(att[:, 0:features], wo[:, cols], preferred_element_type=jnp.float32)
        resid[:, cols] = tokens[:, cols].astype(jnp.float32) + value
    norm_rows(lambda at: resid[at, :], write_acts, 1)
    swap = push(acts.at[pl.ds(0, rows_here)], acts.at[pl.ds(rows_here, rows_here)], partner)
    settled = [0]

    def settle(count=None):
        stop = len(final) if count is None else settled[0] + count
        arrived(final[settled[0] : stop])
        settled[0] = stop

    service_second(1)
    pass_on(2)
    settle(8)
    acc[...] = jnp.zeros_like(acc)
    swap.wait_recv()

    def before_1():
        pass_on(4)

    def before_4():
        settle()

    def before_5():
        service_second(3)

    def before_6():
        service_last(0)
        pass_on(4)
        settle()

    def before_7():
        pass_on(2)

    def before_9():
        settle()

    def before_10():
        service_second(2)

    def before_11():
        pass_on(4)
        service_last(1)
        pass_on(2)
        settle()

    def before_12():
        service_last(3)

    def before_13():
        pass_on(2)
        settle()

    def before_14():
        service_last(2)

    def before_15():
        pass_on(2)
        settle()

    order = [
        (0, 0), (1, 0), (3, 0), (0, 1), (0, 3), (1, 1), (1, 3), (3, 1),
        (3, 3), (2, 0), (0, 2), (1, 2), (2, 1), (3, 2), (2, 3), (2, 2),
    ]
    services = {
        1: before_1, 4: before_4, 5: before_5, 6: before_6, 7: before_7, 9: before_9,
        10: before_10, 11: before_11, 12: before_12, 13: before_13, 14: before_14, 15: before_15,
    }

    def ffn(t, carry):
        code = zero
        for n, (i, k) in enumerate(order):
            code = jnp.where(t == n, i * 4 + k, code)
        i, k = code // 4, code % 4
        pre = lax.dot_general(acts[...], wa[k, i], contract, preferred_element_type=jnp.float32)
        hidden = (0.5 * pre * (1.0 + lax.erf(pre * math.sqrt(0.5)))).astype(jnp.bfloat16)
        for start, width in ((0, 512), (512, 512), (1024, 384)):
            acc[:, start : start + width] += jnp.dot(
                hidden, wb[k, i, :, start : start + width], preferred_element_type=jnp.float32
            )
        return carry

    begun = 0
    for n in [*sorted(services), len(order)]:
        lax.fori_loop(begun, n, ffn, 0)
        if n in services:
            services[n]()
        begun = n

    def narrow(t, carry):
        at = pl.multiple_of(t * 32, 32)
        psend[pl.ds(at, 32), :] = acc[pl.ds(rows_here + at, 32), :].astype(jnp.bfloat16)
        return carry

    lax.fori_loop(0, rows_here // 32, narrow, 0)
    back = push(psend, precv, partner)
    back.wait_recv()

    def write_att(at, value):
        att[at, 0:features] = value.astype(jnp.bfloat16)

    norm_rows(
        lambda at: resid[at, :] + (acc[at, :] + precv[at, :].astype(jnp.float32)), write_att, 2
    )
    for q in range(4):
        merged_out[:, q * features : (q + 1) * features] = jnp.dot(
            pick[q], att[:, 0:features], preferred_element_type=jnp.float32
        ).astype(jnp.bfloat16)
    for copy in sent:
        copy.wait_send()


def layer(tokens, gain, bias, wq, bq, wo, wa, wb, seg, grid):
    rows_here, features = tokens.shape
    vmem = pl.BlockSpec(memory_space=pltpu.VMEM)
    hbm = pl.BlockSpec(memory_space=pl.ANY)
    copies = 2 * (2 + 2 + 16) + 90 + 2
    return pl.pallas_call(
        layer_kernel,
        out_shape=jax.ShapeDtypeStruct((MERGED_DEV, 4 * features), jnp.bfloat16),
        in_specs=[
            vmem, vmem, vmem, hbm, vmem, hbm, hbm, hbm, vmem,
            pl.BlockSpec(memory_space=pltpu.SMEM),
        ],
        out_specs=vmem,
        scratch_shapes=[
            pltpu.VMEM((4, 4, SLOT, features), jnp.bfloat16),
            pltpu.VMEM((4, 4, SLOT, features), jnp.bfloat16),
            pltpu.VMEM((features, 3 * features), jnp.bfloat16),
            pltpu.VMEM((features, features), jnp.bfloat16),
            pltpu.VMEM((rows_here, 3 * features + 128), jnp.bfloat16),
            pltpu.VMEM((2 * rows_here, features), jnp.bfloat16),
            pltpu.VMEM((rows_here, features), jnp.float32),
            pltpu.VMEM((2 * rows_here, features), jnp.float32),
            pltpu.VMEM((rows_here, features + 128), jnp.bfloat16),
            pltpu.VMEM((rows_here, rows_here), jnp.float32),
            pltpu.VMEM((4, MERGED_DEV, rows_here), jnp.bfloat16),
            pltpu.VMEM((rows_here, features), jnp.bfloat16),
            pltpu.VMEM((rows_here, features), jnp.bfloat16),
            pltpu.SemaphoreType.DMA((copies,)),
            pltpu.SemaphoreType.DMA((copies,)),
            pltpu.SemaphoreType.DMA((22,)),
        ],
        compiler_params=pltpu.CompilerParams(
            collective_id=1, has_side_effects=True, vmem_limit_bytes=60 * 1024 * 1024
        ),
        name="layer",
    )(tokens, gain, bias, wq, bq, wo, wa, wb, seg, grid)


def merger_kernel(
    merged, w_hbm, gain, grid, routes, outgoing, peaks,
    blocks, weight, acc, req, scaled, stats, gathered, send, recv, local,
):
    row = lax.axis_index("rows")
    member = lax.axis_index("mlp")
    y, core = member // 2, member % 2
    parts = 4
    depth = w_hbm.shape[0] // parts
    group = 8 * MERGED_DEV

    def at_y(dy, other=False):
        side = 1 - core if other else core
        return ((y + dy + 4) % 4) * 2 + side

    started = []
    for q in range(parts):
        copy = pltpu.make_async_copy(
            merged.at[:, pl.ds(q * depth, depth)], blocks.at[q, member], local.at[q]
        )
        copy.start()
        started.append(copy)
    fetched = []
    for q in range(parts):
        rows_q = pl.ds(q * depth, depth)
        copy = pltpu.make_async_copy(w_hbm.at[rows_q], weight.at[rows_q], local.at[parts + q])
        copy.start()
        fetched.append(copy)

    barrier = pltpu.get_barrier_semaphore()
    for step in range(1, 8):
        pl.semaphore_signal(
            barrier, inc=1, device_id=(row, (member + step) % 8), device_id_type=MESH
        )
    pl.semaphore_wait(barrier, 7)

    sent = []

    def push(src, dst, to):
        k = len(sent)
        copy = pltpu.make_async_remote_copy(
            src_ref=src, dst_ref=dst, send_sem=send.at[k], recv_sem=recv.at[k],
            device_id=(row, to), device_id_type=MESH,
        )
        copy.start()
        sent.append(copy)
        return copy

    half = MERGED_DEV // 2
    up, low = pl.ds(0, half), pl.ds(half, half)
    first = []
    for q in range(parts):
        started[q].wait()
        mine = blocks.at[q, member]
        first.append([push(mine, mine, at_y(1)), push(mine, mine, at_y(-1))])
    swap = []
    for q in range(parts):
        mine = blocks.at[q, member]
        swap.append([push(mine, mine, at_y(0, True))])

    target_row = routes[...]
    target_col = jnp.broadcast_to(target_row.astype(jnp.float32), (128, group)).T.astype(jnp.int32)
    rank = jnp.zeros((1, group), jnp.int32)
    for t in range(4):
        here = lax.broadcasted_iota(jnp.int32, (128, group), 0) + 128 * t
        there = lax.broadcasted_iota(jnp.int32, (128, group), 1)
        same = (target_col[128 * t : 128 * (t + 1), 0:1] == target_row) & (here < there)
        rank = rank + jnp.sum(jnp.where(same, 1, 0), axis=0, keepdims=True)
    key = target_row * 8 + rank

    lane_row = lax.broadcasted_iota(jnp.int32, (1, 128), 1)
    number = jnp.zeros((1, 128), jnp.int32)
    slot = lax.broadcasted_iota(jnp.int32, (MERGED_DEV, 128), 0)
    for t in range(8):
        owner = jnp.full((MERGED_DEV, 128), 128, jnp.int32)
        for k, (_, _, _, merge, count) in enumerate(request_spans(grid, t * REQ_DEV)):
            here = (slot >= merge) & (slot < merge + count)
            owner = jnp.where(here, t * REQ_DEV + k, owner)
            number = jnp.where(lane_row == t * REQ_DEV + k, count, number)
        req[t * MERGED_DEV : (t + 1) * MERGED_DEV, :] = owner
    number = number.astype(jnp.float32)

    across = []
    for q in range(parts + 1):
        if q < parts:
            below = blocks.at[q, at_y(-1)]
            above = blocks.at[q, at_y(1)]
            first[q][0].wait_recv()
            across_q = [push(below.at[up], below.at[up], at_y(1))]
            swap[q].append(push(below, below, at_y(0, True)))
            first[q][1].wait_recv()
            across_q.append(push(above.at[low], above.at[low], at_y(-1)))
            swap[q].append(push(above, above, at_y(0, True)))
            across.append(across_q)
        if q >= 1:
            p = q - 1
            far = blocks.at[p, at_y(2)]
            across[p][0].wait_recv()
            across[p][1].wait_recv()
            swap[p].append(push(far, far, at_y(0, True)))
            fetched[p].wait()
            for copy in swap[p]:
                copy.wait_recv()

            def column(n, carry, p=p):
                cols = pl.ds(pl.multiple_of(n * 256, 256), 256)
                value = jnp.dot(
                    blocks[p].reshape(group, depth),
                    weight[p * depth : (p + 1) * depth, cols],
                    preferred_element_type=jnp.float32,
                )
                if p == 0:
                    acc[:, cols] = value
                else:
                    acc[:, cols] += value
                return carry

            lax.fori_loop(0, acc.shape[1] // 256, column, 0)

    lane = lax.broadcasted_iota(jnp.int32, (MERGED_DEV, 128), 1)
    gain_row = gain[...].reshape(1, acc.shape[1])

    def tally(t, carry):
        sums, tops = carry
        at = pl.ds(pl.multiple_of(t * MERGED_DEV, MERGED_DEV), MERGED_DEV)
        value = acc[at, :]
        squares = jnp.sum(value * value, axis=1, keepdims=True)
        top = jnp.max(value * gain_row, axis=1, keepdims=True)
        owns = req[at, :] == lane
        sums = sums + jnp.sum(jnp.where(owns, squares, 0.0), axis=0, keepdims=True)
        tops = jnp.maximum(tops, jnp.max(jnp.where(owns, top, -jnp.inf), axis=0, keepdims=True))
        return sums, tops

    sums, tops = lax.fori_loop(
        0, 8, tally, (jnp.zeros((1, 128), jnp.float32), jnp.full((1, 128), -jnp.inf, jnp.float32))
    )
    place = lax.broadcasted_iota(jnp.int32, (8, 128), 0)
    both = jnp.where(place == 0, sums, tops)
    stats[...] = both
    gathered[member] = both
    told = [push(stats, gathered.at[member], (member + step) % 8) for step in range(1, 8)]
    for copy in told:
        copy.wait_recv()
    total = gathered[0, 0:1, :]
    top = gathered[0, 1:2, :]
    for m in range(1, 8):
        total = total + gathered[m, 0:1, :]
        top = jnp.maximum(top, gathered[m, 1:2, :])
    inv_rms = lax.rsqrt(total / (jnp.maximum(number, 1.0) * OUT) + EPS)
    peaks[...] = jnp.where(number > 0.0, top * inv_rms, 0.0)

    def scale(t, carry):
        at = pl.ds(pl.multiple_of(t * MERGED_DEV, MERGED_DEV), MERGED_DEV)
        row_inv = jnp.sum(jnp.where(req[at, :] == lane, inv_rms, 0.0), axis=1, keepdims=True)
        scaled[at, :] = (acc[at, :] * gain_row * row_inv).astype(jnp.bfloat16)
        return carry

    lax.fori_loop(0, 8, scale, 0)

    def route(t, carry):
        at = pl.multiple_of(t * 256, 256)
        slot = lax.broadcasted_iota(jnp.int32, (256, group), 0) + at
        pick = (slot == key).astype(jnp.bfloat16)
        outgoing[pl.ds(at, 256), :] = jnp.dot(
            pick, scaled[...], preferred_element_type=jnp.float32
        ).astype(jnp.bfloat16)
        return carry

    lax.fori_loop(0, outgoing.shape[0] // 256, route, 0)
    for copy in sent:
        copy.wait_send()


def merger(merged, weight, gain, grid, routes):
    vmem = pl.BlockSpec(memory_space=pltpu.VMEM)
    hbm = pl.BlockSpec(memory_space=pl.ANY)
    depth, width = weight.shape
    group = 8 * MERGED_DEV
    copies = 32 + 7
    return pl.pallas_call(
        merger_kernel,
        out_shape=(
            jax.ShapeDtypeStruct((1024, width), jnp.bfloat16),
            jax.ShapeDtypeStruct((1, 128), jnp.float32),
        ),
        in_specs=[hbm, hbm, vmem, pl.BlockSpec(memory_space=pltpu.SMEM), vmem],
        out_specs=(vmem, vmem),
        scratch_shapes=[
            pltpu.VMEM((4, 8, MERGED_DEV, depth // 4), jnp.bfloat16),
            pltpu.VMEM((depth, width), jnp.bfloat16),
            pltpu.VMEM((group, width), jnp.float32),
            pltpu.VMEM((group, 128), jnp.int32),
            pltpu.VMEM((group, width), jnp.bfloat16),
            pltpu.VMEM((8, 128), jnp.float32),
            pltpu.VMEM((8, 8, 128), jnp.float32),
            pltpu.SemaphoreType.DMA((copies,)),
            pltpu.SemaphoreType.DMA((copies,)),
            pltpu.SemaphoreType.DMA((8,)),
        ],
        compiler_params=pltpu.CompilerParams(
            collective_id=2, has_side_effects=True, vmem_limit_bytes=60 * 1024 * 1024
        ),
        name="merger",
    )(merged, weight, gain, grid, routes)


def per_device(
    tokens,
    norm_gain,
    norm_bias,
    input_weight,
    input_bias,
    output_weight,
    expand_weight,
    reduce_weight,
    merger_weight,
    output_gain,
    segments,
    grid_sides,
    routes,
):
    n_rows = lax.axis_size("rows")
    n_mlp = lax.axis_size("mlp")
    member = lax.axis_index("mlp")
    merged = layer(
        tokens,
        norm_gain,
        norm_bias,
        input_weight,
        input_bias,
        output_weight,
        expand_weight,
        reduce_weight,
        segments,
        grid_sides,
    )
    outgoing, peak_values = merger(
        merged, merger_weight, output_gain, grid_sides, routes.reshape(1, -1)
    )
    peaks_own = lax.dynamic_slice_in_dim(peak_values[0], member * REQ_DEV, REQ_DEV, 0)
    capacity = outgoing.shape[0] // (n_rows * n_mlp)
    outgoing = outgoing.reshape(n_rows * n_mlp, capacity, -1)
    arrived = lax.all_to_all(outgoing, ("rows", "mlp"), split_axis=0, concat_axis=0, tiled=True)
    arrived = arrived.reshape(n_rows, n_mlp, capacity, -1)
    delivered = arrived.transpose(2, 0, 1, 3).reshape(capacity * n_rows, -1)
    return (delivered, peaks_own)


def solution(mesh):
    return jax.shard_map(
        per_device,
        mesh=mesh,
        in_specs=(
            P(("rows", "mlp"), None),
            P(),
            P(),
            P(),
            P(),
            P(),
            P("rows", None),
            P("rows", None),
            P(None, "mlp"),
            P("mlp"),
            P(("rows", "mlp")),
            P("rows", None),
            P("rows", None),
        ),
        out_specs=(P(("rows", "mlp"), None), P(("rows", "mlp"))),
        check_vma=False,
    )
```

```python
import math

import jax
import jax.numpy as jnp
from jax import lax
from jax.experimental import pallas as pl
from jax.experimental.pallas import tpu as pltpu
from jax.sharding import PartitionSpec as P

HEADS = 16
HEAD = 88
OUT = 4096
REQ_DEV = 4
MERGED_DEV = 64


EPS = 1e-06


MESH = pl.DeviceIdType.MESH


def request_spans(grid, first):
    spans = []
    token, merge = 0, 0
    for k in range(REQ_DEV):
        height, width = grid[0, first + k], grid[1, first + k]
        count = lax.div(height, 2) * lax.div(width, 2)
        spans.append((height, width, token, merge, count))
        token = token + jnp.where(height > 0, 1 + height * width, 0)
        merge = merge + count
    return spans


PLANE = 144
HALF = 80
SHARE = 16
SLOT = 192


def layer_kernel(
    tokens, gain, bias, wq_hbm, bq, wo_hbm, wa_hbm, wb_hbm, seg, grid, merged_out,
    wa, wb, wq, wo, joint, acts, resid, acc, att, maskb, pick, psend, precv,
    send, recv, local,
):
    row = lax.axis_index("rows")
    member = lax.axis_index("mlp")
    x, z = row // 4, row % 4
    y, core = member // 2, member % 2
    zero = row - row
    features = tokens.shape[1]
    rows_here = tokens.shape[0]

    def plane(dx, dz):
        return (((x + dx + 4) % 4) * 4 + (z + dz + 4) % 4, member)

    def column(dy):
        return (row, ((y + dy + 4) % 4) * 2 + core)

    partner = (row, member + 1 - 2 * core)
    near = [plane(1, 0), plane(-1, 0), plane(0, 1), plane(0, -1), column(1), column(-1), partner]

    started = []

    def load(src, dst):
        copy = pltpu.make_async_copy(src, dst, local.at[len(started)])
        copy.start()
        started.append(copy)
        return copy

    own = []
    first = SLOT - 4 * SHARE
    for hbm, vmem in ((wa_hbm, wa), (wb_hbm, wb)):
        base = pl.multiple_of(core * SLOT, 16)
        own.append(load(hbm.at[pl.ds(base, first)], vmem.at[0, 0, pl.ds(0, first)]))
        for place, offset in enumerate((0, -1, 1, 2)):
            at = pl.multiple_of(core * SLOT + first + SHARE * ((y + offset + 4) % 4), 16)
            own.append(
                load(hbm.at[pl.ds(at, SHARE)], vmem.at[0, 0, pl.ds(first + place * SHARE, SHARE)])
            )
    chunk = 384
    parts = wq_hbm.shape[1] // chunk
    first_wq = len(started)
    for j in range(parts):
        load(wq_hbm.at[:, pl.ds(j * chunk, chunk)], wq.at[:, pl.ds(j * chunk, chunk)])
    wo_copy = load(wo_hbm, wo)

    barrier = pltpu.get_barrier_semaphore()
    for device in near:
        pl.semaphore_signal(barrier, inc=1, device_id=device, device_id_type=MESH)
    pl.semaphore_wait(barrier, len(near))

    sent = []

    def push(src, dst, device):
        k = len(sent)
        copy = pltpu.make_async_remote_copy(
            src_ref=src, dst_ref=dst, send_sem=send.at[k], recv_sem=recv.at[k],
            device_id=device, device_id_type=MESH,
        )
        copy.start()
        sent.append(copy)
        return copy

    def slot_a(i, k):
        return wa.at[k, i]

    def slot_b(i, k):
        return wb.at[i, k]

    def step_x(s):
        return plane(s, 0)

    def step_z(s):
        return plane(0, s)

    weights = ((slot_a, step_x, step_z), (slot_b, step_z, step_x))
    up, low, whole = pl.ds(0, HALF), pl.ds(HALF, PLANE - HALF), pl.ds(0, PLANE)

    def send_first(w):
        slot, one, _ = w
        return [
            push(slot(0, 0).at[whole], slot(3, 0).at[whole], one(1)),
            push(slot(0, 0).at[whole], slot(1, 0).at[whole], one(-1)),
        ]

    def forward_first(w):
        slot, one, _ = w
        return [
            push(slot(3, 0).at[up], slot(2, 0).at[up], one(1)),
            push(slot(1, 0).at[low], slot(2, 0).at[low], one(-1)),
        ]

    def send_second(w, i):
        slot, _, two = w
        return [
            push(slot(i, 0).at[whole], slot(i, 3).at[whole], two(1)),
            push(slot(i, 0).at[whole], slot(i, 1).at[whole], two(-1)),
        ]

    def forward_second(w, i):
        slot, _, two = w
        return [
            push(slot(i, 3).at[up], slot(i, 2).at[up], two(1)),
            push(slot(i, 1).at[low], slot(i, 2).at[low], two(-1)),
        ]

    share = [pl.ds(first + j * SHARE, SHARE) for j in range(4)]

    def share_out(w, i, k):
        slot = w[0]
        return [
            push(slot(i, k).at[share[0]], slot(i, k).at[share[1]], column(1)),
            push(slot(i, k).at[share[0]], slot(i, k).at[share[2]], column(-1)),
        ]

    def share_on(w, i, k):
        slot = w[0]
        if (i + k) % 2 == 0:
            return push(slot(i, k).at[share[1]], slot(i, k).at[share[3]], column(1))
        return push(slot(i, k).at[share[2]], slot(i, k).at[share[3]], column(-1))

    def arrived(copies):
        for copy in copies:
            copy.wait_recv()

    for copy in own:
        copy.wait()
    table = {}
    for n, w in enumerate(weights):
        table["s1", n] = send_first(w)
    for n, w in enumerate(weights):
        table["s2", n, 0] = send_second(w, 0)

    passing = []

    def spread(slots):
        for n, i, k in slots:
            passing.append((n, i, k, share_out(weights[n], i, k)))

    final = []

    def pass_on(count):
        for _ in range(min(count, len(passing))):
            n, i, k, copies = passing.pop(0)
            arrived(copies)
            final.append(share_on(weights[n], i, k))

    def service_first():
        for n in (0, 1):
            arrived(table["s1", n])
        for n in (0, 1):
            table["f1", n] = forward_first(weights[n])
        for n in (0, 1):
            for i in (1, 3):
                table["s2", n, i] = send_second(weights[n], i)
        spread([(n, i, 0) for n in (0, 1) for i in (1, 3)])

    def service_second(i):
        for n in (0, 1):
            arrived(table["s2", n, i])
            table["f2", n, i] = forward_second(weights[n], i)
        spread([(n, i, k) for n in (0, 1) for k in (1, 3)])

    def service_across():
        for n in (0, 1):
            arrived(table["f1", n])
            table["s2", n, 2] = send_second(weights[n], 2)
        spread([(n, 2, 0) for n in (0, 1)])

    def service_last(i):
        for n in (0, 1):
            arrived(table["f2", n, i])
        spread([(n, i, 2) for n in (0, 1)])

    def norm_rows(read, write, i):
        def body(t, carry):
            at = pl.ds(pl.multiple_of(t * 32, 32), 32)
            value = read(at)
            mean = jnp.mean(value, axis=-1, keepdims=True)
            centered = value - mean
            variance = jnp.mean(centered * centered, axis=-1, keepdims=True)
            write(at, centered * lax.rsqrt(variance + EPS) * gain[i : i + 1, :] + bias[i : i + 1, :])
            return carry

        lax.fori_loop(0, rows_here // 32, body, 0, unroll=2)

    def write_acts(at, value):
        acts[at, :] = value.astype(jnp.bfloat16)

    norm_rows(lambda at: tokens[at, :].astype(jnp.float32), write_acts, 0)
    seg_f = jnp.broadcast_to(
        seg[...].astype(jnp.float32).reshape(1, rows_here), (rows_here, rows_here)
    )
    maskb[...] = jnp.where(seg_f == seg_f.T, 0.0, -jnp.inf)
    joint[:, parts * chunk :] = jnp.zeros((rows_here, joint.shape[1] - parts * chunk), jnp.bfloat16)
    att[...] = jnp.zeros_like(att)

    def pick_rows():
        slot = lax.broadcasted_iota(jnp.int32, (MERGED_DEV, rows_here), 0)
        place = lax.broadcasted_iota(jnp.int32, (MERGED_DEV, rows_here), 1)
        corner = jnp.full((MERGED_DEV, rows_here), -1000, jnp.int32)
        wide = jnp.zeros((MERGED_DEV, rows_here), jnp.int32)
        for _, width, token, merge, count in request_spans(grid, member * REQ_DEV):
            within = slot - merge
            half = lax.div(width, 2)
            line = jnp.zeros_like(within)
            for n in range(1, 4):
                line = line + jnp.where(within >= n * half, 1, 0)
            at = token + 1 + 2 * line * width + 2 * (within - line * half)
            here = (within >= 0) & (within < count)
            corner = jnp.where(here, at, corner)
            wide = jnp.where(here, width, wide)
        one, none = jnp.ones((), jnp.float32), jnp.zeros((), jnp.float32)
        for q in range(4):
            at = corner + (q % 2) + (wide if q >= 2 else 0)
            pick[q] = jnp.where(at == place, one, none).astype(jnp.bfloat16)

    def project(j, carry):
        cols = pl.ds(pl.multiple_of(j * chunk, chunk), chunk)
        pltpu.make_async_copy(wq_hbm.at[:, cols], wq.at[:, cols], local.at[first_wq + j]).wait()
        value = jnp.dot(acts[0:rows_here, :], wq[:, cols], preferred_element_type=jnp.float32)
        joint[:, cols] = (value + bq[cols].reshape(1, chunk)).astype(jnp.bfloat16)
        return carry

    lax.fori_loop(0, parts, project, 0)
    service_first()
    pick_rows()

    contract = (((1,), (1,)), ((), ()))

    def head(h, carry):
        start = (h * HEAD) // 128 * 128
        lead = h * HEAD - start
        lane = lax.broadcasted_iota(jnp.int32, (1, 256), 1)
        inside = (lane >= lead) & (lane < lead + HEAD)
        q = joint[:, pl.ds(pl.multiple_of(start, 128), 256)]
        k = joint[:, pl.ds(pl.multiple_of(features + start, 128), 256)]
        v = joint[:, pl.ds(pl.multiple_of(2 * features + start, 128), 256)]
        zero = jnp.zeros_like(k)
        k = jnp.where(inside, k, zero)
        v = jnp.where(inside, v, zero)
        scores = lax.dot_general(q, k, contract, preferred_element_type=jnp.float32)
        scores = scores / math.sqrt(HEAD) + maskb[...]
        top = jnp.max(scores, axis=-1, keepdims=True)
        weights_ = jnp.exp(scores - top)
        total = jnp.sum(weights_, axis=-1, keepdims=True)
        soft = (weights_ * (1.0 / total)).astype(jnp.bfloat16)
        mixed = jnp.dot(soft, v, preferred_element_type=jnp.float32)
        into = pl.ds(pl.multiple_of(start, 128), 256)
        att[:, into] = att[:, into] + mixed.astype(jnp.bfloat16)
        return carry

    lax.fori_loop(0, 6, head, 0, unroll=2)
    pass_on(4)
    lax.fori_loop(6, 10, head, 0, unroll=2)
    service_second(0)
    lax.fori_loop(10, 16, head, 0, unroll=2)
    service_across()
    pass_on(4)

    wo_copy.wait()
    for start, width in ((0, 512), (512, 512), (1024, 384)):
        cols = slice(start, start + width)
        value = jnp.dot(att[:, 0:features], wo[:, cols], preferred_element_type=jnp.float32)
        resid[:, cols] = tokens[:, cols].astype(jnp.float32) + value
    norm_rows(lambda at: resid[at, :], write_acts, 1)
    swap = push(acts.at[pl.ds(0, rows_here)], acts.at[pl.ds(rows_here, rows_here)], partner)
    settled = [0]

    def settle(count=None):
        stop = len(final) if count is None else settled[0] + count
        arrived(final[settled[0] : stop])
        settled[0] = stop

    service_second(1)
    pass_on(2)
    settle(8)
    acc[...] = jnp.zeros_like(acc)
    swap.wait_recv()

    def before_1():
        pass_on(4)

    def before_4():
        settle()

    def before_5():
        service_second(3)

    def before_6():
        service_last(0)
        pass_on(4)
        settle()

    def before_7():
        pass_on(2)

    def before_9():
        settle()

    def before_10():
        service_second(2)

    def before_11():
        pass_on(4)
        service_last(1)
        pass_on(2)
        settle()

    def before_12():
        service_last(3)

    def before_13():
        pass_on(2)
        settle()

    def before_14():
        service_last(2)

    def before_15():
        pass_on(2)
        settle()

    order = [
        (0, 0), (1, 0), (3, 0), (0, 1), (0, 3), (1, 1), (1, 3), (3, 1),
        (3, 3), (2, 0), (0, 2), (1, 2), (2, 1), (3, 2), (2, 3), (2, 2),
    ]
    services = {
        1: before_1, 4: before_4, 5: before_5, 6: before_6, 7: before_7, 9: before_9,
        10: before_10, 11: before_11, 12: before_12, 13: before_13, 14: before_14, 15: before_15,
    }

    def ffn(t, carry):
        code = zero
        for n, (i, k) in enumerate(order):
            code = jnp.where(t == n, i * 4 + k, code)
        i, k = code // 4, code % 4
        pre = lax.dot_general(acts[...], wa[k, i], contract, preferred_element_type=jnp.float32)
        hidden = (0.5 * pre * (1.0 + lax.erf(pre * math.sqrt(0.5)))).astype(jnp.bfloat16)
        for start, width in ((0, 512), (512, 512), (1024, 384)):
            acc[:, start : start + width] += jnp.dot(
                hidden, wb[k, i, :, start : start + width], preferred_element_type=jnp.float32
            )
        return carry

    begun = 0
    for n in [*sorted(services), len(order)]:
        lax.fori_loop(begun, n, ffn, 0)
        if n in services:
            services[n]()
        begun = n

    def narrow(t, carry):
        at = pl.multiple_of(t * 32, 32)
        psend[pl.ds(at, 32), :] = acc[pl.ds(rows_here + at, 32), :].astype(jnp.bfloat16)
        return carry

    lax.fori_loop(0, rows_here // 32, narrow, 0)
    back = push(psend, precv, partner)
    back.wait_recv()

    def write_att(at, value):
        att[at, 0:features] = value.astype(jnp.bfloat16)

    norm_rows(
        lambda at: resid[at, :] + (acc[at, :] + precv[at, :].astype(jnp.float32)), write_att, 2
    )
    for q in range(4):
        merged_out[:, q * features : (q + 1) * features] = jnp.dot(
            pick[q], att[:, 0:features], preferred_element_type=jnp.float32
        ).astype(jnp.bfloat16)
    for copy in sent:
        copy.wait_send()


def layer(tokens, gain, bias, wq, bq, wo, wa, wb, seg, grid):
    rows_here, features = tokens.shape
    vmem = pl.BlockSpec(memory_space=pltpu.VMEM)
    hbm = pl.BlockSpec(memory_space=pl.ANY)
    copies = 2 * (2 + 2 + 16) + 90 + 2
    return pl.pallas_call(
        layer_kernel,
        out_shape=jax.ShapeDtypeStruct((MERGED_DEV, 4 * features), jnp.bfloat16),
        in_specs=[
            vmem, vmem, vmem, hbm, vmem, hbm, hbm, hbm, vmem,
            pl.BlockSpec(memory_space=pltpu.SMEM),
        ],
        out_specs=vmem,
        scratch_shapes=[
            pltpu.VMEM((4, 4, SLOT, features), jnp.bfloat16),
            pltpu.VMEM((4, 4, SLOT, features), jnp.bfloat16),
            pltpu.VMEM((features, 3 * features), jnp.bfloat16),
            pltpu.VMEM((features, features), jnp.bfloat16),
            pltpu.VMEM((rows_here, 3 * features + 128), jnp.bfloat16),
            pltpu.VMEM((2 * rows_here, features), jnp.bfloat16),
            pltpu.VMEM((rows_here, features), jnp.float32),
            pltpu.VMEM((2 * rows_here, features), jnp.float32),
            pltpu.VMEM((rows_here, features + 128), jnp.bfloat16),
            pltpu.VMEM((rows_here, rows_here), jnp.float32),
            pltpu.VMEM((4, MERGED_DEV, rows_here), jnp.bfloat16),
            pltpu.VMEM((rows_here, features), jnp.bfloat16),
            pltpu.VMEM((rows_here, features), jnp.bfloat16),
            pltpu.SemaphoreType.DMA((copies,)),
            pltpu.SemaphoreType.DMA((copies,)),
            pltpu.SemaphoreType.DMA((22,)),
        ],
        compiler_params=pltpu.CompilerParams(
            collective_id=1, has_side_effects=True, vmem_limit_bytes=60 * 1024 * 1024
        ),
        name="layer",
    )(tokens, gain, bias, wq, bq, wo, wa, wb, seg, grid)


def merger_kernel(
    merged, w_hbm, gain, grid, routes, inbox, peaks,
    blocks, weight, acc, req, scaled, stats, gathered, outgoing, send, recv, local,
    post, mail, entered,
):
    row = lax.axis_index("rows")
    member = lax.axis_index("mlp")
    y, core = member // 2, member % 2
    parts = 4
    depth = w_hbm.shape[0] // parts
    group = 8 * MERGED_DEV

    def at_y(dy, other=False):
        side = 1 - core if other else core
        return ((y + dy + 4) % 4) * 2 + side

    started = []
    for q in range(parts):
        copy = pltpu.make_async_copy(
            merged.at[:, pl.ds(q * depth, depth)], blocks.at[q, member], local.at[q]
        )
        copy.start()
        started.append(copy)
    fetched = []
    for q in range(parts):
        rows_q = pl.ds(q * depth, depth)
        copy = pltpu.make_async_copy(w_hbm.at[rows_q], weight.at[rows_q], local.at[parts + q])
        copy.start()
        fetched.append(copy)

    barrier = pltpu.get_barrier_semaphore()
    for step in range(1, 8):
        pl.semaphore_signal(
            barrier, inc=1, device_id=(row, (member + step) % 8), device_id_type=MESH
        )
    for step in range(1, 16):
        pl.semaphore_signal(
            barrier, inc=1, device_id=((row + step) % 16, member), device_id_type=MESH
        )
    pl.semaphore_wait(barrier, 22)
    for step in range(1, 16):
        pl.semaphore_signal(
            entered, inc=1, device_id=((row + step) % 16, member), device_id_type=MESH
        )

    sent = []

    def push(src, dst, to):
        k = len(sent)
        copy = pltpu.make_async_remote_copy(
            src_ref=src, dst_ref=dst, send_sem=send.at[k], recv_sem=recv.at[k],
            device_id=(row, to), device_id_type=MESH,
        )
        copy.start()
        sent.append(copy)
        return copy

    half = MERGED_DEV // 2
    up, low = pl.ds(0, half), pl.ds(half, half)
    first = []
    for q in range(parts):
        started[q].wait()
        mine = blocks.at[q, member]
        first.append([push(mine, mine, at_y(1)), push(mine, mine, at_y(-1))])
    swap = []
    for q in range(parts):
        mine = blocks.at[q, member]
        swap.append([push(mine, mine, at_y(0, True))])

    target_row = routes[...]
    target_col = jnp.broadcast_to(target_row.astype(jnp.float32), (128, group)).T.astype(jnp.int32)
    rank = jnp.zeros((1, group), jnp.int32)
    for t in range(4):
        here = lax.broadcasted_iota(jnp.int32, (128, group), 0) + 128 * t
        there = lax.broadcasted_iota(jnp.int32, (128, group), 1)
        same = (target_col[128 * t : 128 * (t + 1), 0:1] == target_row) & (here < there)
        rank = rank + jnp.sum(jnp.where(same, 1, 0), axis=0, keepdims=True)
    key = target_row * 8 + rank

    lane_row = lax.broadcasted_iota(jnp.int32, (1, 128), 1)
    number = jnp.zeros((1, 128), jnp.int32)
    slot = lax.broadcasted_iota(jnp.int32, (MERGED_DEV, 128), 0)
    for t in range(8):
        owner = jnp.full((MERGED_DEV, 128), 128, jnp.int32)
        for k, (_, _, _, merge, count) in enumerate(request_spans(grid, t * REQ_DEV)):
            here = (slot >= merge) & (slot < merge + count)
            owner = jnp.where(here, t * REQ_DEV + k, owner)
            number = jnp.where(lane_row == t * REQ_DEV + k, count, number)
        req[t * MERGED_DEV : (t + 1) * MERGED_DEV, :] = owner
    number = number.astype(jnp.float32)

    across = []
    for q in range(parts + 1):
        if q < parts:
            below = blocks.at[q, at_y(-1)]
            above = blocks.at[q, at_y(1)]
            first[q][0].wait_recv()
            across_q = [push(below.at[up], below.at[up], at_y(1))]
            swap[q].append(push(below, below, at_y(0, True)))
            first[q][1].wait_recv()
            across_q.append(push(above.at[low], above.at[low], at_y(-1)))
            swap[q].append(push(above, above, at_y(0, True)))
            across.append(across_q)
        if q >= 1:
            p = q - 1
            far = blocks.at[p, at_y(2)]
            across[p][0].wait_recv()
            across[p][1].wait_recv()
            swap[p].append(push(far, far, at_y(0, True)))
            fetched[p].wait()
            for copy in swap[p]:
                copy.wait_recv()

            def column(n, carry, p=p):
                cols = pl.ds(pl.multiple_of(n * 256, 256), 256)
                value = jnp.dot(
                    blocks[p].reshape(group, depth),
                    weight[p * depth : (p + 1) * depth, cols],
                    preferred_element_type=jnp.float32,
                )
                if p == 0:
                    acc[:, cols] = value
                else:
                    acc[:, cols] += value
                return carry

            lax.fori_loop(0, acc.shape[1] // 256, column, 0)

    lane = lax.broadcasted_iota(jnp.int32, (MERGED_DEV, 128), 1)
    gain_row = gain[...].reshape(1, acc.shape[1])

    def tally(t, carry):
        sums, tops = carry
        at = pl.ds(pl.multiple_of(t * MERGED_DEV, MERGED_DEV), MERGED_DEV)
        value = acc[at, :]
        squares = jnp.sum(value * value, axis=1, keepdims=True)
        top = jnp.max(value * gain_row, axis=1, keepdims=True)
        owns = req[at, :] == lane
        sums = sums + jnp.sum(jnp.where(owns, squares, 0.0), axis=0, keepdims=True)
        tops = jnp.maximum(tops, jnp.max(jnp.where(owns, top, -jnp.inf), axis=0, keepdims=True))
        return sums, tops

    sums, tops = lax.fori_loop(
        0, 8, tally, (jnp.zeros((1, 128), jnp.float32), jnp.full((1, 128), -jnp.inf, jnp.float32))
    )
    place = lax.broadcasted_iota(jnp.int32, (8, 128), 0)
    both = jnp.where(place == 0, sums, tops)
    stats[...] = both
    gathered[member] = both
    told = [push(stats, gathered.at[member], (member + step) % 8) for step in range(1, 8)]
    for copy in told:
        copy.wait_recv()
    total = gathered[0, 0:1, :]
    top = gathered[0, 1:2, :]
    for m in range(1, 8):
        total = total + gathered[m, 0:1, :]
        top = jnp.maximum(top, gathered[m, 1:2, :])
    inv_rms = lax.rsqrt(total / (jnp.maximum(number, 1.0) * OUT) + EPS)
    highest = jnp.where(number > 0.0, top * inv_rms, 0.0)
    own_slots = pltpu.roll(jnp.broadcast_to(highest, (8, 128)), (128 - member * REQ_DEV) % 128, 1)
    peaks[...] = own_slots[0, 0:REQ_DEV]

    def scale(t, carry):
        at = pl.ds(pl.multiple_of(t * MERGED_DEV, MERGED_DEV), MERGED_DEV)
        row_inv = jnp.sum(jnp.where(req[at, :] == lane, inv_rms, 0.0), axis=1, keepdims=True)
        scaled[at, :] = (acc[at, :] * gain_row * row_inv).astype(jnp.bfloat16)
        return carry

    lax.fori_loop(0, 8, scale, 0)

    me = row * 8 + member
    here_x = row // 4

    def route(t):
        first = (here_x + t) % 4 * 32
        slot = lax.broadcasted_iota(jnp.int32, (256, group), 0) + first * 8
        pick = (slot == key).astype(jnp.bfloat16)
        outgoing[pl.ds(first, 32)] = jnp.dot(
            pick, scaled[...], preferred_element_type=jnp.float32
        ).astype(jnp.bfloat16).reshape(32, 8, acc.shape[1])

    def letter(t, n):
        to = (here_x + t) % 4 * 32 + (me % 32 + n) % 32
        return pltpu.make_async_remote_copy(
            src_ref=outgoing.at[to], dst_ref=inbox.at[me],
            send_sem=post.at[t * 32 + n], recv_sem=mail.at[t * 32 + n],
            device_id=(to // 8, to % 8), device_id_type=MESH,
        )

    def mail_out(t):
        def body(n, carry):
            letter(t, n).start()
            return carry

        lax.fori_loop(1 if t == 0 else 0, 32, body, 0)

    route(1)
    pl.semaphore_wait(entered, 15)
    for n, t in enumerate((1, 3, 2, 0)):
        if n < 3:
            route((3, 2, 0)[n])
        mail_out(t)
    keep = pltpu.make_async_copy(outgoing.at[me], inbox.at[me], local.at[0])
    keep.start()
    for t in (1, 3, 2, 0):
        def settle(n, carry, t=t):
            copy = letter(t, n)
            copy.wait_send()
            copy.wait_recv()
            return carry

        lax.fori_loop(1 if t == 0 else 0, 32, settle, 0)
    keep.wait()
    for copy in sent:
        copy.wait_send()


def merger(merged, weight, gain, grid, routes):
    vmem = pl.BlockSpec(memory_space=pltpu.VMEM)
    hbm = pl.BlockSpec(memory_space=pl.ANY)
    depth, width = weight.shape
    group = 8 * MERGED_DEV
    copies = 32 + 7
    return pl.pallas_call(
        merger_kernel,
        out_shape=(
            jax.ShapeDtypeStruct((128, 8, width), jnp.bfloat16),
            jax.ShapeDtypeStruct((REQ_DEV,), jnp.float32),
        ),
        in_specs=[hbm, hbm, vmem, pl.BlockSpec(memory_space=pltpu.SMEM), vmem],
        out_specs=(hbm, vmem),
        scratch_shapes=[
            pltpu.VMEM((4, 8, MERGED_DEV, depth // 4), jnp.bfloat16),
            pltpu.VMEM((depth, width), jnp.bfloat16),
            pltpu.VMEM((group, width), jnp.float32),
            pltpu.VMEM((group, 128), jnp.int32),
            pltpu.VMEM((group, width), jnp.bfloat16),
            pltpu.VMEM((8, 128), jnp.float32),
            pltpu.VMEM((8, 8, 128), jnp.float32),
            pltpu.VMEM((128, 8, width), jnp.bfloat16),
            pltpu.SemaphoreType.DMA((copies,)),
            pltpu.SemaphoreType.DMA((copies,)),
            pltpu.SemaphoreType.DMA((8,)),
            pltpu.SemaphoreType.DMA((128,)),
            pltpu.SemaphoreType.DMA((128,)),
            pltpu.SemaphoreType.REGULAR,
        ],
        compiler_params=pltpu.CompilerParams(
            collective_id=2, has_side_effects=True, vmem_limit_bytes=60 * 1024 * 1024
        ),
        name="merger",
    )(merged, weight, gain, grid, routes)


def per_device(
    tokens,
    norm_gain,
    norm_bias,
    input_weight,
    input_bias,
    output_weight,
    expand_weight,
    reduce_weight,
    merger_weight,
    output_gain,
    segments,
    grid_sides,
    routes,
):
    n_rows = lax.axis_size("rows")
    n_mlp = lax.axis_size("mlp")
    sides = grid_sides.T
    merged = layer(
        tokens,
        norm_gain,
        norm_bias,
        input_weight,
        input_bias,
        output_weight,
        expand_weight,
        reduce_weight,
        segments,
        sides,
    )
    arrived, peaks_own = merger(
        merged, merger_weight, output_gain, sides, routes.reshape(1, -1)
    )
    arrived = arrived.reshape(n_rows, n_mlp, arrived.shape[1], -1)
    delivered = arrived.transpose(2, 0, 1, 3).reshape(arrived.shape[2] * n_rows, -1)
    return (delivered, peaks_own)


def solution(mesh):
    return jax.shard_map(
        per_device,
        mesh=mesh,
        in_specs=(
            P(("rows", "mlp"), None),
            P(),
            P(),
            P(),
            P(),
            P(),
            P("rows", None),
            P("rows", None),
            P(None, "mlp"),
            P("mlp"),
            P(("rows", "mlp")),
            P("rows", None),
            P("rows", None),
        ),
        out_specs=(P(("rows", "mlp"), None), P(("rows", "mlp"))),
        check_vma=False,
    )
```

```python
import math

import jax
import jax.numpy as jnp
from jax import lax
from jax.experimental import pallas as pl
from jax.experimental.pallas import tpu as pltpu
from jax.sharding import PartitionSpec as P

HEADS = 16
HEAD = 88
OUT = 4096
REQ_DEV = 4
MERGED_DEV = 64


EPS = 1e-06


MESH = pl.DeviceIdType.MESH


def request_spans(grid, first):
    spans = []
    token, merge = 0, 0
    for k in range(REQ_DEV):
        height, width = grid[0, first + k], grid[1, first + k]
        count = lax.div(height, 2) * lax.div(width, 2)
        spans.append((height, width, token, merge, count))
        token = token + jnp.where(height > 0, 1 + height * width, 0)
        merge = merge + count
    return spans


PLANE = 144
HALF = 80
SHARE = 16
SLOT = 192


def layer_kernel(
    tokens, gain, bias, wq_hbm, bq, wo_hbm, wa_hbm, wb_hbm, seg, grid, w_hbm,
    wa, wb, wq, wo, joint, acts, resid, acc, att, maskb, pick, psend, precv,
    send, recv, local, blocks, entered,
):
    row = lax.axis_index("rows")
    member = lax.axis_index("mlp")
    x, z = row // 4, row % 4
    y, core = member // 2, member % 2
    zero = row - row
    features = tokens.shape[1]
    rows_here = tokens.shape[0]

    def plane(dx, dz):
        return (((x + dx + 4) % 4) * 4 + (z + dz + 4) % 4, member)

    def column(dy):
        return (row, ((y + dy + 4) % 4) * 2 + core)

    partner = (row, member + 1 - 2 * core)
    row_peers = [((row + step) % 16, member) for step in range(1, 16)]
    near = [(row, (member + step) % 8) for step in range(1, 8)] + row_peers

    started = []

    def load(src, dst):
        copy = pltpu.make_async_copy(src, dst, local.at[len(started)])
        copy.start()
        started.append(copy)
        return copy

    own = []
    first = SLOT - 4 * SHARE
    for hbm, vmem in ((wa_hbm, wa), (wb_hbm, wb)):
        base = pl.multiple_of(core * SLOT, 16)
        own.append(load(hbm.at[pl.ds(base, first)], vmem.at[0, 0, pl.ds(0, first)]))
        for place, offset in enumerate((0, -1, 1, 2)):
            at = pl.multiple_of(core * SLOT + first + SHARE * ((y + offset + 4) % 4), 16)
            own.append(
                load(hbm.at[pl.ds(at, SHARE)], vmem.at[0, 0, pl.ds(first + place * SHARE, SHARE)])
            )
    chunk = 384
    parts = wq_hbm.shape[1] // chunk
    first_wq = len(started)
    for j in range(parts):
        load(wq_hbm.at[:, pl.ds(j * chunk, chunk)], wq.at[:, pl.ds(j * chunk, chunk)])
    wo_copy = load(wo_hbm, wo)

    barrier = pltpu.get_barrier_semaphore()
    for device in near:
        pl.semaphore_signal(barrier, inc=1, device_id=device, device_id_type=MESH)
    pl.semaphore_wait(barrier, len(near))

    sent = []

    def push(src, dst, device):
        k = len(sent)
        copy = pltpu.make_async_remote_copy(
            src_ref=src, dst_ref=dst, send_sem=send.at[k], recv_sem=recv.at[k],
            device_id=device, device_id_type=MESH,
        )
        copy.start()
        sent.append(copy)
        return copy

    def slot_a(i, k):
        return wa.at[k, i]

    def slot_b(i, k):
        return wb.at[i, k]

    def step_x(s):
        return plane(s, 0)

    def step_z(s):
        return plane(0, s)

    weights = ((slot_a, step_x, step_z), (slot_b, step_z, step_x))
    up, low, whole = pl.ds(0, HALF), pl.ds(HALF, PLANE - HALF), pl.ds(0, PLANE)

    def send_first(w):
        slot, one, _ = w
        return [
            push(slot(0, 0).at[whole], slot(3, 0).at[whole], one(1)),
            push(slot(0, 0).at[whole], slot(1, 0).at[whole], one(-1)),
        ]

    def forward_first(w):
        slot, one, _ = w
        return [
            push(slot(3, 0).at[up], slot(2, 0).at[up], one(1)),
            push(slot(1, 0).at[low], slot(2, 0).at[low], one(-1)),
        ]

    def send_second(w, i):
        slot, _, two = w
        return [
            push(slot(i, 0).at[whole], slot(i, 3).at[whole], two(1)),
            push(slot(i, 0).at[whole], slot(i, 1).at[whole], two(-1)),
        ]

    def forward_second(w, i):
        slot, _, two = w
        return [
            push(slot(i, 3).at[up], slot(i, 2).at[up], two(1)),
            push(slot(i, 1).at[low], slot(i, 2).at[low], two(-1)),
        ]

    share = [pl.ds(first + j * SHARE, SHARE) for j in range(4)]

    def share_out(w, i, k):
        slot = w[0]
        return [
            push(slot(i, k).at[share[0]], slot(i, k).at[share[1]], column(1)),
            push(slot(i, k).at[share[0]], slot(i, k).at[share[2]], column(-1)),
        ]

    def share_on(w, i, k):
        slot = w[0]
        if (i + k) % 2 == 0:
            return push(slot(i, k).at[share[1]], slot(i, k).at[share[3]], column(1))
        return push(slot(i, k).at[share[2]], slot(i, k).at[share[3]], column(-1))

    def arrived(copies):
        for copy in copies:
            copy.wait_recv()

    for copy in own:
        copy.wait()
    table = {}
    for n, w in enumerate(weights):
        table["s1", n] = send_first(w)
    for n, w in enumerate(weights):
        table["s2", n, 0] = send_second(w, 0)
    for device in row_peers:
        pl.semaphore_signal(entered, inc=1, device_id=device, device_id_type=MESH)

    passing = []

    def spread(slots):
        for n, i, k in slots:
            passing.append((n, i, k, share_out(weights[n], i, k)))

    final = []

    def pass_on(count):
        for _ in range(min(count, len(passing))):
            n, i, k, copies = passing.pop(0)
            arrived(copies)
            final.append(share_on(weights[n], i, k))

    def service_first():
        for n in (0, 1):
            arrived(table["s1", n])
        for n in (0, 1):
            table["f1", n] = forward_first(weights[n])
        for n in (0, 1):
            for i in (1, 3):
                table["s2", n, i] = send_second(weights[n], i)
        spread([(n, i, 0) for n in (0, 1) for i in (1, 3)])

    def service_second(i):
        for n in (0, 1):
            arrived(table["s2", n, i])
            table["f2", n, i] = forward_second(weights[n], i)
        spread([(n, i, k) for n in (0, 1) for k in (1, 3)])

    def service_across():
        for n in (0, 1):
            arrived(table["f1", n])
            table["s2", n, 2] = send_second(weights[n], 2)
        spread([(n, 2, 0) for n in (0, 1)])

    def service_last(i):
        for n in (0, 1):
            arrived(table["f2", n, i])
        spread([(n, i, 2) for n in (0, 1)])

    def norm_rows(read, write, i, begin=0, end=rows_here):
        def body(t, carry):
            at = pl.ds(pl.multiple_of(t * 32, 32), 32)
            value = read(at)
            mean = jnp.mean(value, axis=-1, keepdims=True)
            centered = value - mean
            variance = jnp.mean(centered * centered, axis=-1, keepdims=True)
            write(at, centered * lax.rsqrt(variance + EPS) * gain[i : i + 1, :] + bias[i : i + 1, :])
            return carry

        lax.fori_loop(begin // 32, end // 32, body, 0, unroll=2)

    def write_acts(at, value):
        acts[at, :] = value.astype(jnp.bfloat16)

    norm_rows(lambda at: tokens[at, :].astype(jnp.float32), write_acts, 0)
    seg_f = jnp.broadcast_to(
        seg[...].astype(jnp.float32).reshape(1, rows_here), (rows_here, rows_here)
    )
    maskb[...] = jnp.where(seg_f == seg_f.T, 0.0, -jnp.inf)
    joint[:, parts * chunk :] = jnp.zeros((rows_here, joint.shape[1] - parts * chunk), jnp.bfloat16)
    att[...] = jnp.zeros_like(att)

    def pick_rows():
        slot = lax.broadcasted_iota(jnp.int32, (MERGED_DEV, rows_here), 0)
        place = lax.broadcasted_iota(jnp.int32, (MERGED_DEV, rows_here), 1)
        corner = jnp.full((MERGED_DEV, rows_here), -1000, jnp.int32)
        wide = jnp.zeros((MERGED_DEV, rows_here), jnp.int32)
        for _, width, token, merge, count in request_spans(grid, member * REQ_DEV):
            within = slot - merge
            half = lax.div(width, 2)
            line = jnp.zeros_like(within)
            for n in range(1, 4):
                line = line + jnp.where(within >= n * half, 1, 0)
            at = token + 1 + 2 * line * width + 2 * (within - line * half)
            here = (within >= 0) & (within < count)
            corner = jnp.where(here, at, corner)
            wide = jnp.where(here, width, wide)
        one, none = jnp.ones((), jnp.float32), jnp.zeros((), jnp.float32)
        for q in range(4):
            at = corner + (q % 2) + (wide if q >= 2 else 0)
            pick[q] = jnp.where(at == place, one, none).astype(jnp.bfloat16)

    def project(j, carry):
        cols = pl.ds(pl.multiple_of(j * chunk, chunk), chunk)
        pltpu.make_async_copy(wq_hbm.at[:, cols], wq.at[:, cols], local.at[first_wq + j]).wait()
        value = jnp.dot(acts[0:rows_here, :], wq[:, cols], preferred_element_type=jnp.float32)
        joint[:, cols] = (value + bq[cols].reshape(1, chunk)).astype(jnp.bfloat16)
        return carry

    lax.fori_loop(0, parts, project, 0)
    service_first()
    width = w_hbm.shape[1]
    fetched = [
        load(w_hbm.at[pl.ds(q * features, features)], wq.at[:, pl.ds(q * width, width)])
        for q in range(4)
    ]
    pick_rows()

    contract = (((1,), (1,)), ((), ()))

    def head(h, carry):
        start = (h * HEAD) // 128 * 128
        lead = h * HEAD - start
        lane = lax.broadcasted_iota(jnp.int32, (1, 256), 1)
        inside = (lane >= lead) & (lane < lead + HEAD)
        q = joint[:, pl.ds(pl.multiple_of(start, 128), 256)]
        k = joint[:, pl.ds(pl.multiple_of(features + start, 128), 256)]
        v = joint[:, pl.ds(pl.multiple_of(2 * features + start, 128), 256)]
        zero = jnp.zeros_like(k)
        k = jnp.where(inside, k, zero)
        v = jnp.where(inside, v, zero)
        scores = lax.dot_general(q, k, contract, preferred_element_type=jnp.float32)
        scores = scores / math.sqrt(HEAD) + maskb[...]
        top = jnp.max(scores, axis=-1, keepdims=True)
        weights_ = jnp.exp(scores - top)
        total = jnp.sum(weights_, axis=-1, keepdims=True)
        soft = (weights_ * (1.0 / total)).astype(jnp.bfloat16)
        mixed = jnp.dot(soft, v, preferred_element_type=jnp.float32)
        into = pl.ds(pl.multiple_of(start, 128), 256)
        att[:, into] = att[:, into] + mixed.astype(jnp.bfloat16)
        return carry

    lax.fori_loop(0, 6, head, 0, unroll=2)
    pass_on(4)
    lax.fori_loop(6, 10, head, 0, unroll=2)
    service_second(0)
    lax.fori_loop(10, 16, head, 0, unroll=2)
    service_across()
    pass_on(4)

    wo_copy.wait()
    for start, width in ((0, 512), (512, 512), (1024, 384)):
        cols = slice(start, start + width)
        value = jnp.dot(att[:, 0:features], wo[:, cols], preferred_element_type=jnp.float32)
        resid[:, cols] = tokens[:, cols].astype(jnp.float32) + value
    norm_rows(lambda at: resid[at, :], write_acts, 1)
    swap = push(acts.at[pl.ds(0, rows_here)], acts.at[pl.ds(rows_here, rows_here)], partner)
    settled = [0]

    def settle(count=None):
        stop = len(final) if count is None else settled[0] + count
        arrived(final[settled[0] : stop])
        settled[0] = stop

    service_second(1)
    pass_on(2)
    settle(8)
    acc[...] = jnp.zeros_like(acc)
    swap.wait_recv()

    def before_1():
        pass_on(4)

    def before_4():
        settle()

    def before_5():
        service_second(3)

    def before_6():
        service_last(0)
        pass_on(4)
        settle()

    def before_7():
        pass_on(2)

    def before_9():
        settle()

    def before_10():
        service_second(2)

    def before_11():
        pass_on(4)
        service_last(1)
        pass_on(2)
        settle()

    def before_12():
        service_last(3)

    def before_13():
        pass_on(2)
        settle()

    def before_14():
        service_last(2)

    def before_15():
        pass_on(2)
        settle()

    order = [
        (0, 0), (1, 0), (3, 0), (0, 1), (0, 3), (1, 1), (1, 3), (3, 1),
        (3, 3), (2, 0), (0, 2), (1, 2), (2, 1), (3, 2), (2, 3), (2, 2),
    ]
    services = {
        1: before_1, 4: before_4, 5: before_5, 6: before_6, 7: before_7, 9: before_9,
        10: before_10, 11: before_11, 12: before_12, 13: before_13, 14: before_14, 15: before_15,
    }

    def ffn_rows(i, k, begin, end):
        pre = lax.dot_general(acts[begin:end, :], wa[k, i], contract, preferred_element_type=jnp.float32)
        hidden = (0.5 * pre * (1.0 + lax.erf(pre * math.sqrt(0.5)))).astype(jnp.bfloat16)
        for start, width in ((0, 512), (512, 512), (1024, 384)):
            acc[begin:end, start : start + width] += jnp.dot(
                hidden, wb[k, i, :, start : start + width], preferred_element_type=jnp.float32
            )

    def ffn(t, carry):
        code = zero
        for n, (i, k) in enumerate(order):
            code = jnp.where(t == n, i * 4 + k, code)
        i, k = code // 4, code % 4
        ffn_rows(i, k, 0, 2 * rows_here)
        return carry

    begun = 0
    for n in sorted(services):
        lax.fori_loop(begun, n, ffn, 0)
        if n in services:
            services[n]()
        begun = n

    def narrow(t, carry):
        at = pl.multiple_of(t * 32, 32)
        psend[pl.ds(at, 32), :] = acc[pl.ds(rows_here + at, 32), :].astype(jnp.bfloat16)
        return carry

    last_i, last_k = order[-1]
    ffn_rows(last_i, last_k, rows_here, 2 * rows_here)
    piece = rows_here // 4
    back = []

    def hand_over(p):
        at = pl.ds(p * piece, piece)
        back.append(push(psend.at[at], precv.at[at], partner))

    for p in range(4):
        lax.fori_loop(p * piece // 32, (p + 1) * piece // 32, narrow, 0)
        if p >= 1:
            hand_over(p - 1)
    hand_over(3)
    ffn_rows(last_i, last_k, 0, rows_here)

    def write_att(at, value):
        att[at, 0:features] = value.astype(jnp.bfloat16)

    for p in range(4):
        back[p].wait_recv()
        norm_rows(
            lambda at: resid[at, :] + (acc[at, :] + precv[at, :].astype(jnp.float32)),
            write_att, 2, p * piece, (p + 1) * piece,
        )

    def produce(q):
        blocks[q, member] = jnp.dot(
            pick[q], att[:, 0:features], preferred_element_type=jnp.float32
        ).astype(jnp.bfloat16)

    return produce, fetched, sent


def merger_kernel(
    produce, fetched, gain, grid, routes, inbox, peaks,
    blocks, weight, acc, req, scaled, stats, gathered, outgoing, send, recv, local,
    post, mail, entered,
):
    row = lax.axis_index("rows")
    member = lax.axis_index("mlp")
    y, core = member // 2, member % 2
    parts = 4
    depth, width = blocks.shape[3], acc.shape[1]
    group = 8 * MERGED_DEV

    def at_y(dy, other=False):
        side = 1 - core if other else core
        return ((y + dy + 4) % 4) * 2 + side

    sent = []

    def push(src, dst, to):
        k = len(sent)
        copy = pltpu.make_async_remote_copy(
            src_ref=src, dst_ref=dst, send_sem=send.at[k], recv_sem=recv.at[k],
            device_id=(row, to), device_id_type=MESH,
        )
        copy.start()
        sent.append(copy)
        return copy

    half = MERGED_DEV // 2
    up, low = pl.ds(0, half), pl.ds(half, half)
    first, swap = [], []
    produce(0)
    for q in range(parts):
        if q + 1 < parts:
            produce(q + 1)
        mine = blocks.at[q, member]
        first.append([push(mine, mine, at_y(1)), push(mine, mine, at_y(-1))])
        swap.append([push(mine, mine, at_y(0, True))])

    target_row = routes[...]
    target_col = jnp.broadcast_to(target_row.astype(jnp.float32), (128, group)).T.astype(jnp.int32)
    rank = jnp.zeros((1, group), jnp.int32)
    for t in range(4):
        here = lax.broadcasted_iota(jnp.int32, (128, group), 0) + 128 * t
        there = lax.broadcasted_iota(jnp.int32, (128, group), 1)
        same = (target_col[128 * t : 128 * (t + 1), 0:1] == target_row) & (here < there)
        rank = rank + jnp.sum(jnp.where(same, 1, 0), axis=0, keepdims=True)
    key = target_row * 8 + rank

    lane_row = lax.broadcasted_iota(jnp.int32, (1, 128), 1)
    number = jnp.zeros((1, 128), jnp.int32)
    slot = lax.broadcasted_iota(jnp.int32, (MERGED_DEV, 128), 0)
    for t in range(8):
        owner = jnp.full((MERGED_DEV, 128), 128, jnp.int32)
        for k, (_, _, _, merge, count) in enumerate(request_spans(grid, t * REQ_DEV)):
            here = (slot >= merge) & (slot < merge + count)
            owner = jnp.where(here, t * REQ_DEV + k, owner)
            number = jnp.where(lane_row == t * REQ_DEV + k, count, number)
        req[t * MERGED_DEV : (t + 1) * MERGED_DEV, :] = owner
    number = number.astype(jnp.float32)

    across = []
    for q in range(parts + 1):
        if q < parts:
            below = blocks.at[q, at_y(-1)]
            above = blocks.at[q, at_y(1)]
            first[q][0].wait_recv()
            across_q = [push(below.at[up], below.at[up], at_y(1))]
            swap[q].append(push(below, below, at_y(0, True)))
            first[q][1].wait_recv()
            across_q.append(push(above.at[low], above.at[low], at_y(-1)))
            swap[q].append(push(above, above, at_y(0, True)))
            across.append(across_q)
        if q >= 1:
            p = q - 1
            far = blocks.at[p, at_y(2)]
            across[p][0].wait_recv()
            across[p][1].wait_recv()
            swap[p].append(push(far, far, at_y(0, True)))
            fetched[p].wait()
            for copy in swap[p]:
                copy.wait_recv()

            def column(n, carry, p=p):
                cols = pl.ds(pl.multiple_of(n * 256, 256), 256)
                value = jnp.dot(
                    blocks[p].reshape(group, depth),
                    weight[:, pl.ds(pl.multiple_of(p * width + n * 256, 256), 256)],
                    preferred_element_type=jnp.float32,
                )
                if p == 0:
                    acc[:, cols] = value
                else:
                    acc[:, cols] += value
                return carry

            lax.fori_loop(0, acc.shape[1] // 256, column, 0)

    lane = lax.broadcasted_iota(jnp.int32, (MERGED_DEV, 128), 1)
    gain_row = gain[...].reshape(1, acc.shape[1])

    def tally(t, carry):
        sums, tops = carry
        at = pl.ds(pl.multiple_of(t * MERGED_DEV, MERGED_DEV), MERGED_DEV)
        value = acc[at, :]
        squares = jnp.sum(value * value, axis=1, keepdims=True)
        top = jnp.max(value * gain_row, axis=1, keepdims=True)
        owns = req[at, :] == lane
        sums = sums + jnp.sum(jnp.where(owns, squares, 0.0), axis=0, keepdims=True)
        tops = jnp.maximum(tops, jnp.max(jnp.where(owns, top, -jnp.inf), axis=0, keepdims=True))
        return sums, tops

    sums, tops = lax.fori_loop(
        0, 8, tally, (jnp.zeros((1, 128), jnp.float32), jnp.full((1, 128), -jnp.inf, jnp.float32))
    )
    place = lax.broadcasted_iota(jnp.int32, (8, 128), 0)
    both = jnp.where(place == 0, sums, tops)
    stats[...] = both
    gathered[member] = both
    told = [push(stats, gathered.at[member], (member + step) % 8) for step in range(1, 8)]
    for copy in told:
        copy.wait_recv()
    total = gathered[0, 0:1, :]
    top = gathered[0, 1:2, :]
    for m in range(1, 8):
        total = total + gathered[m, 0:1, :]
        top = jnp.maximum(top, gathered[m, 1:2, :])
    inv_rms = lax.rsqrt(total / (jnp.maximum(number, 1.0) * OUT) + EPS)
    highest = jnp.where(number > 0.0, top * inv_rms, 0.0)
    own_slots = pltpu.roll(jnp.broadcast_to(highest, (8, 128)), (128 - member * REQ_DEV) % 128, 1)
    peaks[...] = own_slots[0, 0:REQ_DEV]

    def scale(t, carry):
        at = pl.ds(pl.multiple_of(t * MERGED_DEV, MERGED_DEV), MERGED_DEV)
        row_inv = jnp.sum(jnp.where(req[at, :] == lane, inv_rms, 0.0), axis=1, keepdims=True)
        scaled[at, :] = (acc[at, :] * gain_row * row_inv).astype(jnp.bfloat16)
        return carry

    lax.fori_loop(0, 8, scale, 0)

    me = row * 8 + member
    here_x = row // 4

    def route(t):
        first = (here_x + t) % 4 * 32
        slot = lax.broadcasted_iota(jnp.int32, (256, group), 0) + first * 8
        pick = (slot == key).astype(jnp.bfloat16)
        outgoing[pl.ds(first, 32)] = jnp.dot(
            pick, scaled[...], preferred_element_type=jnp.float32
        ).astype(jnp.bfloat16).reshape(32, 8, acc.shape[1])

    def letter(t, n):
        to = (here_x + t) % 4 * 32 + (me % 32 + n) % 32
        return pltpu.make_async_remote_copy(
            src_ref=outgoing.at[to], dst_ref=inbox.at[me],
            send_sem=post.at[t * 32 + n], recv_sem=mail.at[t * 32 + n],
            device_id=(to // 8, to % 8), device_id_type=MESH,
        )

    def mail_out(t):
        def body(n, carry):
            letter(t, n).start()
            return carry

        lax.fori_loop(1 if t == 0 else 0, 32, body, 0)

    route(1)
    pl.semaphore_wait(entered, 15)
    for n, t in enumerate((1, 3, 2, 0)):
        if n < 3:
            route((3, 2, 0)[n])
        mail_out(t)
    keep = pltpu.make_async_copy(outgoing.at[me], inbox.at[me], local.at[0])
    keep.start()
    for t in (1, 3, 2, 0):
        def settle(n, carry, t=t):
            copy = letter(t, n)
            copy.wait_send()
            copy.wait_recv()
            return carry

        lax.fori_loop(1 if t == 0 else 0, 32, settle, 0)
    keep.wait()
    for copy in sent:
        copy.wait_send()


def whole_kernel(
    tokens, gain, bias, wq_hbm, bq, wo_hbm, wa_hbm, wb_hbm, seg, grid, w_hbm, out_gain, routes,
    inbox, peaks, *scratch,
):
    wq, blocks, entered = scratch[2], scratch[16], scratch[17]
    produce, fetched, sent = layer_kernel(
        tokens, gain, bias, wq_hbm, bq, wo_hbm, wa_hbm, wb_hbm, seg, grid, w_hbm, *scratch[:18]
    )
    merger_kernel(
        produce, fetched, out_gain, grid, routes, inbox, peaks,
        blocks, wq, *scratch[18:], entered,
    )
    for copy in sent:
        copy.wait_send()


def whole(tokens, gain, bias, wq, bq, wo, wa, wb, seg, grid, weight, out_gain, routes):
    rows_here, features = tokens.shape
    vmem = pl.BlockSpec(memory_space=pltpu.VMEM)
    hbm = pl.BlockSpec(memory_space=pl.ANY)
    smem = pl.BlockSpec(memory_space=pltpu.SMEM)
    width = weight.shape[1]
    group = 8 * MERGED_DEV
    copies = 2 * (2 + 2 + 16) + 90 + 5
    merger_copies = 32 + 7
    return pl.pallas_call(
        whole_kernel,
        out_shape=(
            jax.ShapeDtypeStruct((128, 8, width), jnp.bfloat16),
            jax.ShapeDtypeStruct((REQ_DEV,), jnp.float32),
        ),
        in_specs=[
            vmem, vmem, vmem, hbm, vmem, hbm, hbm, hbm, vmem, smem, hbm, vmem, vmem,
        ],
        out_specs=(hbm, vmem),
        scratch_shapes=[
            pltpu.VMEM((4, 4, SLOT, features), jnp.bfloat16),
            pltpu.VMEM((4, 4, SLOT, features), jnp.bfloat16),
            pltpu.VMEM((features, 3 * features), jnp.bfloat16),
            pltpu.VMEM((features, features), jnp.bfloat16),
            pltpu.VMEM((rows_here, 3 * features + 128), jnp.bfloat16),
            pltpu.VMEM((2 * rows_here, features), jnp.bfloat16),
            pltpu.VMEM((rows_here, features), jnp.float32),
            pltpu.VMEM((2 * rows_here, features), jnp.float32),
            pltpu.VMEM((rows_here, features + 128), jnp.bfloat16),
            pltpu.VMEM((rows_here, rows_here), jnp.float32),
            pltpu.VMEM((4, MERGED_DEV, rows_here), jnp.bfloat16),
            pltpu.VMEM((rows_here, features), jnp.bfloat16),
            pltpu.VMEM((rows_here, features), jnp.bfloat16),
            pltpu.SemaphoreType.DMA((copies,)),
            pltpu.SemaphoreType.DMA((copies,)),
            pltpu.SemaphoreType.DMA((26,)),
            pltpu.VMEM((4, 8, MERGED_DEV, features), jnp.bfloat16),
            pltpu.SemaphoreType.REGULAR,
            pltpu.VMEM((group, width), jnp.float32),
            pltpu.VMEM((group, 128), jnp.int32),
            pltpu.VMEM((group, width), jnp.bfloat16),
            pltpu.VMEM((8, 128), jnp.float32),
            pltpu.VMEM((8, 8, 128), jnp.float32),
            pltpu.VMEM((128, 8, width), jnp.bfloat16),
            pltpu.SemaphoreType.DMA((merger_copies,)),
            pltpu.SemaphoreType.DMA((merger_copies,)),
            pltpu.SemaphoreType.DMA((8,)),
            pltpu.SemaphoreType.DMA((128,)),
            pltpu.SemaphoreType.DMA((128,)),
        ],
        compiler_params=pltpu.CompilerParams(
            collective_id=1, has_side_effects=True, vmem_limit_bytes=60 * 1024 * 1024
        ),
        name="whole",
    )(tokens, gain, bias, wq, bq, wo, wa, wb, seg, grid, weight, out_gain, routes)


def per_device(
    tokens,
    norm_gain,
    norm_bias,
    input_weight,
    input_bias,
    output_weight,
    expand_weight,
    reduce_weight,
    merger_weight,
    output_gain,
    segments,
    grid_sides,
    routes,
):
    n_rows = lax.axis_size("rows")
    n_mlp = lax.axis_size("mlp")
    sides = grid_sides.T
    arrived, peaks_own = whole(
        tokens,
        norm_gain,
        norm_bias,
        input_weight,
        input_bias,
        output_weight,
        expand_weight,
        reduce_weight,
        segments,
        sides,
        merger_weight,
        output_gain,
        routes.reshape(1, -1),
    )
    arrived = arrived.reshape(n_rows, n_mlp, arrived.shape[1], -1)
    delivered = arrived.transpose(2, 0, 1, 3).reshape(arrived.shape[2] * n_rows, -1)
    return (delivered, peaks_own)


def solution(mesh):
    return jax.shard_map(
        per_device,
        mesh=mesh,
        in_specs=(
            P(("rows", "mlp"), None),
            P(),
            P(),
            P(),
            P(),
            P(),
            P("rows", None),
            P("rows", None),
            P(None, "mlp"),
            P("mlp"),
            P(("rows", "mlp")),
            P("rows", None),
            P("rows", None),
        ),
        out_specs=(P(("rows", "mlp"), None), P(("rows", "mlp"))),
        check_vma=False,
    )
```
